128 devices in a mesh: section: 16 (over z_hi, y, core), seq: 8 (over x, z_lo).
Axes of the slice: x: 4, y: 4, z: 4 (z_hi: 2, z_lo: 2; z = z_hi * 2 + z_lo), core: 2. Of those that a mesh axis runs over, the one named last changes fastest.
Arguments:
- forward_rows: bfloat16 [16, 1024, 4096], P('section', 'seq'), may hold values from -54 to 54
- saved_rows: bfloat16 [16, 1024, 4096], P('section', 'seq'), may hold values from -54 to 54
- output_grad: bfloat16 [16, 1024, 4096], P('section', 'seq'), may hold values from -6 to 6
- forward_docs: int32 [16, 1024], replicated, may hold values from 0 to 3, never falling along the last dimension, each value on 1 to 512 neighbouring positions
- backward_docs: int32 [16, 1024], replicated, may hold values from 0 to 3, never falling along the last dimension, each value on 1 to 512 neighbouring positions
- norm_gain: float32 [16, 4096], P('section'), may hold values from 0.7 to 8
- query_weight: bfloat16 [16, 4096, 4096], P('section', None, 'seq'), may hold values from -0.09375 to 0.09375
- key_matrix: bfloat16 [16, 4096, 1024], P('section', None, 'seq'), may hold values from -0.09375 to 0.09375
- value_matrix: bfloat16 [16, 4096, 1024], P('section', None, 'seq'), may hold values from -0.09375 to 0.09375
Outputs:
- section_output: bfloat16 [16, 1024, 4096], P('section', 'seq')
- input_grad: bfloat16 [16, 1024, 4096], P('section', 'seq')
The draws below stay inside these ranges and needn't reach their ends.
Inputs may be any that keep to these rules, and one draw needn't show every extreme that they name: `forward_docs`: document ids never fall along a row; every document holds at most 512 tokens and some document of each row holds exactly that many. `backward_docs`: document ids never fall along a row; every document holds at most 512 tokens and some document of each row holds exactly that many.
All inputs are finite; a program needn't handle non-finite values.
Results may differ from the reference program's by a relative error of at most 0.017.
The reference program's roundings to bfloat16 on the way count: a program that leaves them out, or rounds other values in their place, can miss the bound.
Values may be sent and summed in bfloat16 or wider, within the bound.
A program may use at most 192 MiB of HBM per device.

```python
import math
import jax
import jax.numpy as jnp
import numpy as np
from jax import lax

MODEL_WIDTH = 4096
HQ = 32
KEY_VALUE_HEADS = 8
HEAD_SIZE = 128
QUERIES_PER_KEY = 4
SEQLEN = 1024
N_SECTION = 16
N_SEQ = 8


def scaled_rows(key):
    base_key, col_key, row_key = jax.random.split(key, 3)
    base = jnp.clip(jax.random.normal(base_key, (N_SECTION, SEQLEN, MODEL_WIDTH)), -6.0, 6.0)
    col_scale = jnp.exp(jax.random.uniform(col_key, (N_SECTION, 1, MODEL_WIDTH), minval=math.log(0.3), maxval=math.log(3.0)))
    row_scale = jnp.exp(jax.random.uniform(row_key, (N_SECTION, SEQLEN, 1), minval=math.log(0.3), maxval=math.log(3.0)))
    return (base * col_scale * row_scale).astype(jnp.float32)


def draw_forward_rows(key, part):
    return scaled_rows(jax.random.fold_in(key, 11)).astype(jnp.bfloat16)


def draw_saved_rows(key, part):
    return scaled_rows(jax.random.fold_in(key, 12)).astype(jnp.bfloat16)


def draw_norm_gain(key, part):
    gain_key = jax.random.fold_in(key, 31)
    return (1.0 + 0.3 * jax.random.uniform(gain_key, (N_SECTION, MODEL_WIDTH), minval=-1.0, maxval=1.0)).astype(jnp.float32)


def level_of(rng, shape, cuts, least, largest):
    level = 1.0
    for position, parts in cuts:
        draws = jax.random.uniform(jax.random.fold_in(jax.random.fold_in(rng, 6), position), (parts,), jnp.float32, least / len(cuts), largest / len(cuts))
        level = level * jnp.repeat(jnp.exp(draws), shape[position] // parts).reshape((-1,) + (1,) * (len(shape) - 1 - position))
    return level


def split_up(amount, total, reach, skew):
    portions = [(1 << 20) // math.isqrt(standing ** skew) + 1 for standing in range(2, amount + 1)]
    rest, holding = total - reach - (amount - 1), [1] * (amount - 1)
    while rest > 0:
        free = [i for i in range(amount - 1) if holding[i] < reach]
        whole, left = sum([portions[i] for i in free]), rest
        for i in free:
            more = min(reach - holding[i], max(1, left * portions[i] // whole), rest)
            holding[i] = holding[i] + more
            rest = rest - more
    return np.array([reach] + holding)


def ragged_sizes(stream_key, amount, total, reach, skew):
    if amount == 2:
        one = jax.random.randint(stream_key, (), max(1, total - reach), min(reach, total - 1) + 1)
        return jnp.stack([one, total - one])
    sizes = jnp.asarray(split_up(amount, total, reach, skew), jnp.int32)
    twos = (amount - 1) // 2
    donor, receiver = sizes[1:1 + 2 * twos:2], sizes[2:2 + 2 * twos:2]
    margin = jnp.minimum(donor - 1, reach - receiver)
    shifted = jax.random.randint(jax.random.fold_in(stream_key, 1), (twos,), 0, 1 << 20) % (margin + 1)
    sizes = sizes.at[1:1 + 2 * twos:2].set(donor - shifted).at[2:2 + 2 * twos:2].set(receiver + shifted)
    return sizes[jax.random.permutation(jax.random.fold_in(stream_key, 2), amount)]


def normal_values(stream_key, dims, deviation, limit, cuts=(), held_as=jnp.bfloat16):
    array = jax.random.normal(stream_key, dims, jnp.float32) * deviation
    if len(cuts) > 0:
        array = level_of(stream_key, dims, cuts, -0.22, 0.18) * array
    return jnp.clip(array, min=-limit, max=limit).astype(held_as)


def setup_inputs(seed: int = 0) -> dict:
    splits = jax.random.split(jax.random.key(seed), 10)
    return {
        "forward_rows": draw_forward_rows(jax.random.fold_in(splits[9], 71), 0),
        "saved_rows": draw_saved_rows(jax.random.fold_in(splits[9], 71), 0),
        "output_grad": normal_values(splits[2], (N_SECTION, SEQLEN, MODEL_WIDTH), 1.0, 6.0, ((0, 16), (1, 8))),
        "forward_docs": jax.vmap(lambda own: jnp.searchsorted(jnp.cumsum(ragged_sizes(own, 4, SEQLEN, SEQLEN // 2, 0)), jnp.arange(SEQLEN), side="right"))(jax.random.split(splits[3], N_SECTION)).reshape((N_SECTION, SEQLEN)).astype(jnp.int32),
        "backward_docs": jax.vmap(lambda own: jnp.searchsorted(jnp.cumsum(ragged_sizes(own, 4, SEQLEN, SEQLEN // 2, 0)), jnp.arange(SEQLEN), side="right"))(jax.random.split(splits[4], N_SECTION)).reshape((N_SECTION, SEQLEN)).astype(jnp.int32),
        "norm_gain": draw_norm_gain(jax.random.fold_in(splits[9], 71), 0),
        "query_weight": normal_values(splits[6], (N_SECTION, MODEL_WIDTH, HQ * HEAD_SIZE), MODEL_WIDTH ** -0.5, 0.09375, ((0, 16), (2, 8))),
        "key_matrix": normal_values(splits[7], (N_SECTION, MODEL_WIDTH, KEY_VALUE_HEADS * HEAD_SIZE), MODEL_WIDTH ** -0.5, 0.09375, ((0, 16), (2, 8))),
        "value_matrix": normal_values(splits[8], (N_SECTION, MODEL_WIDTH, KEY_VALUE_HEADS * HEAD_SIZE), MODEL_WIDTH ** -0.5, 0.09375, ((0, 16), (2, 8))),
    }


epsilon = 1e-05
rope_base = 500000.0

def rounded(values):
    return lax.optimization_barrier(values.astype(jnp.bfloat16))

def rotation_tables(positions):
    half = HEAD_SIZE // 2
    freqs = rope_base ** (-(jnp.arange(half, dtype=jnp.float32) * 2.0 / HEAD_SIZE))
    angles = positions[:, None] * freqs[None, :]
    return (jnp.cos(angles), jnp.sin(angles))

def rotate(values, cosines, sines, sign):
    half = values.shape[-1] // 2
    extra = (1,) * (values.ndim - 2)
    cos_wide = cosines.reshape(cosines.shape[:1] + extra + cosines.shape[1:])
    sin_wide = sines.reshape(sines.shape[:1] + extra + sines.shape[1:])
    first = values[..., :half]
    second = values[..., half:]
    return jnp.concatenate([first * cos_wide - sign * second * sin_wide, second * cos_wide + sign * first * sin_wide], axis=-1)

def project(hidden, gain_row, query_weight, key_matrix, value_matrix):
    sequence_length = hidden.shape[0]
    scale_rows = lax.rsqrt(lax.optimization_barrier(jnp.mean(hidden * hidden, axis=-1, keepdims=True)) + epsilon)
    normalized_input = rounded(hidden * scale_rows * gain_row)
    cosines, sines = rotation_tables(jnp.arange(sequence_length, dtype=jnp.float32))
    query_proj = jnp.dot(normalized_input, query_weight, preferred_element_type=jnp.float32).reshape(sequence_length, HQ, HEAD_SIZE)
    key_projected_rows = jnp.dot(normalized_input, key_matrix, preferred_element_type=jnp.float32).reshape(sequence_length, KEY_VALUE_HEADS, HEAD_SIZE)
    value_projected_rows = jnp.dot(normalized_input, value_matrix, preferred_element_type=jnp.float32).reshape(sequence_length, KEY_VALUE_HEADS, HEAD_SIZE)
    query_rows_local = rounded(rotate(query_proj, cosines, sines, 1.0))
    key_rows = rounded(rotate(key_projected_rows, cosines, sines, 1.0))
    value_rows = rounded(value_projected_rows)
    return (scale_rows, query_rows_local, key_rows, value_rows, cosines, sines)

def allowed_pairs(documents):
    sequence_length = documents.shape[0]
    positions = jnp.arange(sequence_length)
    return (positions[None, :] <= positions[:, None]) & (documents[:, None] == documents[None, :])

def group_probs(query_group, key_head, allowed):
    scores = jnp.einsum('tgd,sd->gts', query_group.astype(jnp.float32), key_head.astype(jnp.float32)) * HEAD_SIZE ** (-0.5)
    scores = jnp.where(allowed, scores, -1e+30)
    row_top = lax.optimization_barrier(jnp.max(scores, axis=-1, keepdims=True))
    exp_scores = jnp.where(allowed, jnp.exp(scores - row_top), 0.0)
    return exp_scores / lax.optimization_barrier(jnp.sum(exp_scores, axis=-1, keepdims=True))

def forward_layer(layer_rows, documents, gain_row, query_weight, key_matrix, value_matrix):
    hidden = layer_rows.astype(jnp.float32)
    sequence_length = hidden.shape[0]
    scale_rows, query_rows_local, key_rows, value_rows, cosines, sines = project(hidden, gain_row, query_weight, key_matrix, value_matrix)
    allowed = allowed_pairs(documents)
    query_head_count = query_rows_local.reshape(sequence_length, KEY_VALUE_HEADS, QUERIES_PER_KEY, HEAD_SIZE).transpose(1, 0, 2, 3)
    key_heads = key_rows.transpose(1, 0, 2)
    value_heads = value_rows.transpose(1, 0, 2)

    def one_group(operands):
        query_group, key_head, value_head = operands
        probability = rounded(group_probs(query_group, key_head, allowed))
        return rounded(jnp.einsum('gts,sd->tgd', probability.astype(jnp.float32), value_head.astype(jnp.float32)))
    outputs = lax.map(one_group, (query_head_count, key_heads, value_heads))
    outputs = outputs.transpose(1, 0, 2, 3).reshape(sequence_length, HQ * HEAD_SIZE)
    return (hidden + outputs.astype(jnp.float32)).astype(jnp.bfloat16)

def backward_layer(layer_rows, output_gradient, documents, gain_row, query_weight, key_matrix, value_matrix):
    hidden = layer_rows.astype(jnp.float32)
    sequence_length = hidden.shape[0]
    scale_rows, query_rows_local, key_rows, value_rows, cosines, sines = project(hidden, gain_row, query_weight, key_matrix, value_matrix)
    allowed = allowed_pairs(documents)
    query_head_count = query_rows_local.reshape(sequence_length, KEY_VALUE_HEADS, QUERIES_PER_KEY, HEAD_SIZE).transpose(1, 0, 2, 3)
    key_heads = key_rows.transpose(1, 0, 2)
    value_heads = value_rows.transpose(1, 0, 2)
    head_gradients = output_gradient.reshape(sequence_length, KEY_VALUE_HEADS, QUERIES_PER_KEY, HEAD_SIZE).transpose(1, 0, 2, 3)
    scale = HEAD_SIZE ** (-0.5)

    def one_group(operands):
        query_group, key_head, value_head, grad_group = operands
        probability = group_probs(query_group, key_head, allowed)
        probability_low = rounded(probability).astype(jnp.float32)
        grad_float = grad_group.astype(jnp.float32)
        grad_probs = jnp.einsum('tgd,sd->gts', grad_float, value_head.astype(jnp.float32))
        row_delta = lax.optimization_barrier(jnp.sum(probability * grad_probs, axis=-1, keepdims=True))
        grad_scores = rounded(probability * (grad_probs - row_delta)).astype(jnp.float32)
        query_grad = jnp.einsum('gts,sd->tgd', grad_scores, key_head.astype(jnp.float32)) * scale
        key_grad = jnp.einsum('gts,tgd->sd', grad_scores, query_group.astype(jnp.float32)) * scale
        value_grad = jnp.einsum('gts,tgd->sd', probability_low, grad_float)
        return (rounded(rotate(query_grad, cosines, sines, -1.0)), rounded(rotate(key_grad, cosines, sines, -1.0)), rounded(value_grad))
    query_grads, key_gradient_rows, value_gradient_rows = lax.map(one_group, (query_head_count, key_heads, value_heads, head_gradients))
    query_grads = query_grads.transpose(1, 0, 2, 3).reshape(sequence_length, HQ * HEAD_SIZE)
    key_gradient_rows = key_gradient_rows.transpose(1, 0, 2).reshape(sequence_length, KEY_VALUE_HEADS * HEAD_SIZE)
    value_gradient_rows = value_gradient_rows.transpose(1, 0, 2).reshape(sequence_length, KEY_VALUE_HEADS * HEAD_SIZE)
    query_cols = HQ * HEAD_SIZE // N_SEQ
    pair_columns = KEY_VALUE_HEADS * HEAD_SIZE // N_SEQ
    input_sum = jnp.zeros((sequence_length, MODEL_WIDTH), jnp.float32)
    for index in range(N_SEQ):
        query_slice = slice(index * query_cols, (index + 1) * query_cols)
        pair_slice = slice(index * pair_columns, (index + 1) * pair_columns)
        term = jnp.dot(query_grads[:, query_slice], query_weight[:, query_slice].T, preferred_element_type=jnp.float32)
        term = term + jnp.dot(key_gradient_rows[:, pair_slice], key_matrix[:, pair_slice].T, preferred_element_type=jnp.float32)
        term = term + jnp.dot(value_gradient_rows[:, pair_slice], value_matrix[:, pair_slice].T, preferred_element_type=jnp.float32)
        input_sum = input_sum + rounded(term).astype(jnp.float32)
    gained = gain_row * input_sum
    inner_sum = lax.optimization_barrier(jnp.sum(hidden * gained, axis=-1, keepdims=True))
    norm_part = scale_rows * gained - hidden * (scale_rows * scale_rows * scale_rows) * inner_sum / MODEL_WIDTH
    return (output_gradient.astype(jnp.float32) + norm_part).astype(jnp.bfloat16)

def run_forward(operands):
    layer_rows, documents, gain_row, query_weight, key_matrix, value_matrix = operands
    return forward_layer(layer_rows, documents, gain_row, query_weight, key_matrix, value_matrix)

def run_backward(operands):
    layer_rows, output_gradient, documents, gain_row, query_weight, key_matrix, value_matrix = operands
    return backward_layer(layer_rows, output_gradient, documents, gain_row, query_weight, key_matrix, value_matrix)

def reference(forward_rows, saved_rows, output_grad, forward_docs, backward_docs, norm_gain, query_weight, key_matrix, value_matrix):
    first_out = lax.map(run_forward, (forward_rows, forward_docs, norm_gain, query_weight, key_matrix, value_matrix))
    first_grad = lax.map(run_backward, (saved_rows, output_grad, backward_docs, norm_gain, query_weight, key_matrix, value_matrix))
    empty_rows = jnp.zeros_like(first_out[:1])
    section_output = jnp.concatenate([empty_rows, first_out[:-1]], axis=0)
    input_grad = jnp.concatenate([first_grad[1:], empty_rows], axis=0)
    return (section_output, input_grad)
```

```python
import functools

import jax
import jax.numpy as jnp
from jax import lax
from jax.experimental import pallas as pl
from jax.experimental.pallas import tpu as pltpu
from jax.sharding import PartitionSpec as P

MESH = pl.DeviceIdType.MESH
ROWS = 128
COLS = 4096
HEADS_WIDE = 512
ALL_WIDE = 768

MODEL_WIDTH = 4096
HEAD_SIZE = 128


epsilon = 1e-05
rope_base = 500000.0


def passed_along(shard, axis, by):
    peers = lax.axis_size(axis)
    pairs = [(i, i + by) for i in range(peers) if 0 <= i + by < peers]
    return lax.ppermute(shard, axis, pairs)


def rotation_tables(positions):
    half = HEAD_SIZE // 2
    freqs = rope_base ** (-(jnp.arange(half, dtype=jnp.float32) * 2.0 / HEAD_SIZE))
    angles = positions[:, None] * freqs[None, :]
    return (jnp.cos(angles), jnp.sin(angles))


def rotate(values, cosines, sines, sign):
    half = values.shape[-1] // 2
    extra = (1,) * (values.ndim - 2)
    cos_wide = cosines.reshape(cosines.shape[:1] + extra + cosines.shape[1:])
    sin_wide = sines.reshape(sines.shape[:1] + extra + sines.shape[1:])
    first = values[..., :half]
    second = values[..., half:]
    return jnp.concatenate(
        [first * cos_wide - sign * second * sin_wide, second * cos_wide + sign * first * sin_wide],
        axis=-1,
    )


def pair_mask(row_docs, col_docs, row_begin):
    row_pos = row_begin + lax.iota(jnp.int32, row_docs.shape[0])
    col_pos = lax.iota(jnp.int32, col_docs.shape[0])
    return (col_pos[None, :] <= row_pos[:, None]) & (row_docs[:, None] == col_docs[None, :])


def block_probs(query_block, key_heads, allowed):
    scores = jnp.einsum(
        "tjgd,sjd->jgts", query_block, key_heads, preferred_element_type=jnp.float32
    ) * HEAD_SIZE ** (-0.5)
    scores = jnp.where(allowed, scores, -1e30)
    row_top = jnp.max(scores, axis=-1, keepdims=True)
    exp_scores = jnp.where(allowed, jnp.exp(scores - row_top), 0.0)
    return exp_scores / jnp.sum(exp_scores, axis=-1, keepdims=True)


def attend(query_rows_local, key_rows, value_rows, documents):
    sequence_length = query_rows_local.shape[0]
    groups = key_rows.shape[1] // HEAD_SIZE
    group_size = query_rows_local.shape[1] // key_rows.shape[1]
    query_head_count = query_rows_local.reshape(sequence_length, groups, group_size, HEAD_SIZE)
    key_heads = key_rows.reshape(sequence_length, groups, HEAD_SIZE)
    value_heads = value_rows.reshape(sequence_length, groups, HEAD_SIZE)
    block_rows = min(512, sequence_length)
    pieces = []
    for block_index in range(sequence_length // block_rows):
        begin_row = block_index * block_rows
        end_row = begin_row + block_rows
        allowed = pair_mask(documents[begin_row:end_row], documents[:end_row], begin_row)
        probability = block_probs(
            query_head_count[begin_row:end_row], key_heads[:end_row], allowed
        ).astype(jnp.bfloat16)
        mixed_rows = jnp.einsum(
            "jgts,sjd->tjgd", probability, value_heads[:end_row], preferred_element_type=jnp.float32
        )
        pieces.append(mixed_rows.astype(jnp.bfloat16))
    return lax.optimization_barrier(
        jnp.concatenate(pieces, 0).reshape(sequence_length, query_rows_local.shape[1])
    )


def attend_back(query_rows_local, key_rows, value_rows, output_gradient, documents, cosines, sines):
    sequence_length = query_rows_local.shape[0]
    groups = key_rows.shape[1] // HEAD_SIZE
    group_size = query_rows_local.shape[1] // key_rows.shape[1]
    query_head_count = query_rows_local.reshape(sequence_length, groups, group_size, HEAD_SIZE)
    key_heads = key_rows.reshape(sequence_length, groups, HEAD_SIZE)
    value_heads = value_rows.reshape(sequence_length, groups, HEAD_SIZE)
    head_gradients = output_gradient.reshape(sequence_length, groups, group_size, HEAD_SIZE)
    scale = HEAD_SIZE ** (-0.5)
    key_grad = jnp.zeros((sequence_length, groups, HEAD_SIZE), jnp.float32)
    value_grad = jnp.zeros((sequence_length, groups, HEAD_SIZE), jnp.float32)
    block_rows = min(512, sequence_length)
    query_pieces = []
    for block_index in range(sequence_length // block_rows):
        begin_row = block_index * block_rows
        end_row = begin_row + block_rows
        allowed = pair_mask(documents[begin_row:end_row], documents[:end_row], begin_row)
        query_block = query_head_count[begin_row:end_row]
        grad_block = head_gradients[begin_row:end_row]
        probability = block_probs(query_block, key_heads[:end_row], allowed)
        grad_probs = jnp.einsum(
            "tjgd,sjd->jgts", grad_block, value_heads[:end_row], preferred_element_type=jnp.float32
        )
        row_delta = jnp.sum(probability * grad_probs, axis=-1, keepdims=True)
        grad_scores = (probability * (grad_probs - row_delta)).astype(jnp.bfloat16)
        query_piece = (
            jnp.einsum(
                "jgts,sjd->tjgd",
                grad_scores,
                key_heads[:end_row],
                preferred_element_type=jnp.float32,
            )
            * scale
        )
        query_piece = rotate(
            query_piece, cosines[begin_row:end_row], sines[begin_row:end_row], -1.0
        )
        query_pieces.append(query_piece.astype(jnp.bfloat16))
        key_grad = key_grad.at[:end_row].add(
            jnp.einsum(
                "jgts,tjgd->sjd", grad_scores, query_block, preferred_element_type=jnp.float32
            )
            * scale
        )
        value_grad = value_grad.at[:end_row].add(
            jnp.einsum(
                "jgts,tjgd->sjd",
                probability.astype(jnp.bfloat16),
                grad_block,
                preferred_element_type=jnp.float32,
            )
        )
    query_grad = jnp.concatenate(query_pieces, 0).reshape(
        sequence_length, query_rows_local.shape[1]
    )
    key_grad = (
        rotate(key_grad, cosines, sines, -1.0)
        .astype(jnp.bfloat16)
        .reshape(sequence_length, groups * HEAD_SIZE)
    )
    value_grad = value_grad.astype(jnp.bfloat16).reshape(sequence_length, groups * HEAD_SIZE)
    return lax.optimization_barrier((query_grad, key_grad, value_grad))


def token_scale(hidden):
    return lax.rsqrt(jnp.mean(hidden * hidden, axis=-1, keepdims=True) + epsilon)


def place():
    me = lax.axis_index("seq")
    return me, me // 2, me % 2


def peer_of(x, z):
    return 2 * (x % 4) + z


class Copies:
    def __init__(self, send_sems, recv_sems):
        self.send_sems, self.recv_sems = send_sems, recv_sems
        self.sent = []

    def copy(self, number, src, dst, peer):
        return pltpu.make_async_remote_copy(
            src_ref=src,
            dst_ref=dst,
            send_sem=self.send_sems.at[number],
            recv_sem=self.recv_sems.at[number],
            device_id={"seq": peer},
            device_id_type=MESH,
        )

    def send(self, number, src, dst, peer):
        one = self.copy(number, src, dst, peer)
        one.start()
        self.sent.append(one)

    def arrived(self, number, dst, peer):
        self.copy(number, dst, dst, peer).wait_recv()

    def finish(self):
        for one in self.sent:
            one.wait_send()


def greet(peers):
    barrier = pltpu.get_barrier_semaphore()
    for peer in peers:
        pl.semaphore_signal(barrier, inc=1, device_id={"seq": peer}, device_id_type=MESH)
    pl.semaphore_wait(barrier, len(peers))


def load_weights(weight_refs, whole_weight, sems):
    query_ref, key_ref, value_ref = weight_refs
    copies = [
        pltpu.make_async_copy(query_ref, whole_weight.at[:, 0:512], sems.at[0]),
        pltpu.make_async_copy(key_ref, whole_weight.at[:, 512:640], sems.at[1]),
        pltpu.make_async_copy(value_ref, whole_weight.at[:, 640:768], sems.at[2]),
    ]
    for one in copies:
        one.start()
    return copies


def project_rows(pair, whole, weight, cos_ref, sin_ref, out_ref):
    begin = pl.multiple_of(pair * 256, 256)
    rows = pl.ds(begin, 256)

    @pl.loop(0, 3)
    def _(chunk):
        cols = pl.multiple_of(chunk * 256, 256)
        product = jnp.dot(
            whole[rows, :], weight[:, pl.ds(cols, 256)], preferred_element_type=jnp.float32
        )
        cosines, sines = cos_ref[rows, :], sin_ref[rows, :]
        first, second = product[:, :128], product[:, 128:]
        first_turned = first * cosines + pltpu.roll(first, 64, 1) * sines
        second_turned = second * cosines + pltpu.roll(second, 64, 1) * sines
        second_turned = jnp.where(chunk == 2, second, second_turned)
        out_ref[rows, pl.ds(cols, 128)] = first_turned.astype(jnp.bfloat16)
        out_ref[rows, pl.ds(pl.multiple_of(cols + 128, 128), 128)] = second_turned.astype(
            jnp.bfloat16
        )


def gather_plan(copies, own, whole):
    me, x, z = place()
    right, left, partner = peer_of(x + 1, z), peer_of(x + 3, z), peer_of(x, 1 - z)

    def part(xx, zz, offset, count):
        start = pl.multiple_of(peer_of(xx, zz) * ROWS + offset, 32)
        return whole.at[pl.ds(start, count), :]

    def own_part(offset, count):
        return own.at[pl.ds(offset, count), :]

    def send(number, peer, xx, zz, offset, count):
        copies.send(number, part(xx, zz, offset, count), part(xx, zz, offset, count), peer)

    def got(number, peer, xx, zz, offset, count):
        copies.arrived(number, part(xx, zz, offset, count), peer)

    def begin():
        low, high = own_part(0, 64), own_part(64, 64)
        copies.send(0, low, part(x, z, 0, 64), partner)
        copies.send(6, high, part(x, z, 64, 64), right)
        copies.send(12, high, part(x, z, 64, 64), left)
        copies.send(7, low, part(x, z, 0, 64), right)
        copies.send(13, low, part(x, z, 0, 64), left)
        copies.send(1, high, part(x, z, 64, 64), partner)

    def relay_partner():
        got(0, partner, x, 1 - z, 0, 64)
        send(8, right, x, 1 - z, 0, 64)
        send(14, left, x, 1 - z, 0, 64)

    def relay_high():
        got(6, left, x + 3, z, 64, 64)
        send(9, right, x + 3, z, 64, 32)
        send(2, partner, x + 3, z, 64, 64)
        got(12, right, x + 1, z, 64, 64)
        send(15, left, x + 1, z, 96, 32)
        send(3, partner, x + 1, z, 64, 64)

    def relay_low():
        got(7, left, x + 3, z, 0, 64)
        send(10, right, x + 3, z, 0, 32)
        got(13, right, x + 1, z, 0, 64)
        send(16, left, x + 1, z, 32, 32)

    def own_pair():
        got(1, partner, x, 1 - z, 64, 64)

    def relay_far():
        got(9, left, x + 2, z, 64, 32)
        send(4, partner, x + 2, z, 64, 32)
        got(15, right, x + 2, z, 96, 32)
        send(5, partner, x + 2, z, 96, 32)

    def relay_partner_low():
        got(8, left, x + 3, 1 - z, 0, 64)
        send(11, right, x + 3, 1 - z, 0, 32)
        got(14, right, x + 1, 1 - z, 0, 64)
        send(17, left, x + 1, 1 - z, 32, 32)

    def left_pair():
        got(2, partner, x + 3, 1 - z, 64, 64)

    def right_pair():
        got(3, partner, x + 1, 1 - z, 64, 64)

    def far_pair():
        got(10, left, x + 2, z, 0, 32)
        got(16, right, x + 2, z, 32, 32)
        got(11, left, x + 2, 1 - z, 0, 32)
        got(17, right, x + 2, 1 - z, 32, 32)
        got(4, partner, x + 2, 1 - z, 64, 32)
        got(5, partner, x + 2, 1 - z, 96, 32)

    return (
        begin,
        relay_partner,
        relay_high,
        relay_low,
        own_pair,
        relay_far,
        relay_partner_low,
        left_pair,
        right_pair,
        far_pair,
    )


GATHER_COPIES = 18


def gather_kernel(exchange, *refs):
    if exchange:
        (own, query_ref, key_ref, value_ref, cos_ref, sin_ref, grad_ref, out_ref, heads_ref) = refs[:9]
        refs = refs[9:]
    else:
        (own, query_ref, key_ref, value_ref, cos_ref, sin_ref, out_ref) = refs[:7]
        refs = refs[7:]
    whole, weight, local_sems, send_sems, recv_sems = refs
    me, x, z = place()
    loads = load_weights((query_ref, key_ref, value_ref), weight, local_sems)
    mine = pltpu.make_async_copy(
        own, whole.at[pl.ds(pl.multiple_of(me * ROWS, ROWS), ROWS), :], local_sems.at[3]
    )
    mine.start()
    if exchange:
        peers = [(me + step) % 8 for step in range(1, 8)]
    else:
        peers = [peer_of(x + 1, z), peer_of(x + 3, z), peer_of(x, 1 - z)]
    greet(peers)
    copies = Copies(send_sems, recv_sems)
    (
        begin,
        relay_partner,
        relay_high,
        relay_low,
        own_pair,
        relay_far,
        relay_partner_low,
        left_pair,
        right_pair,
        far_pair,
    ) = gather_plan(copies, own, whole)
    begin()

    def heads_rows(peer):
        return heads_ref.at[pl.ds(pl.multiple_of(peer * ROWS, ROWS), ROWS), :]

    def grad_cols(peer):
        return grad_ref.at[:, pl.ds(pl.multiple_of(peer * HEADS_WIDE, HEADS_WIDE), HEADS_WIDE)]

    if exchange:
        kept = pltpu.make_async_copy(grad_cols(me), heads_rows(me), local_sems.at[4])
        kept.start()
    relay_partner()
    relay_high()
    relay_low()
    if exchange:
        for step in range(1, 8):
            peer = (me + step) % 8
            copies.send(GATHER_COPIES + step - 1, grad_cols(peer), heads_rows(me), peer)
    for one in loads:
        one.wait()
    mine.wait()
    own_pair()
    project_rows(x, whole, weight, cos_ref, sin_ref, out_ref)
    relay_partner_low()
    relay_far()
    left_pair()
    project_rows((x + 3) % 4, whole, weight, cos_ref, sin_ref, out_ref)
    right_pair()
    project_rows((x + 1) % 4, whole, weight, cos_ref, sin_ref, out_ref)
    far_pair()
    project_rows((x + 2) % 4, whole, weight, cos_ref, sin_ref, out_ref)
    if exchange:
        kept.wait()
        for step in range(1, 8):
            peer = (me + 8 - step) % 8
            copies.arrived(GATHER_COPIES + step - 1, heads_rows(peer), peer)
    copies.finish()


def gather_project(own, weights, cosines, sines, collective_id, grad=None):
    exchange = grad is not None
    vmem = pl.BlockSpec(memory_space=pltpu.VMEM)
    anywhere = pl.BlockSpec(memory_space=pl.ANY)
    count = GATHER_COPIES + (7 if exchange else 0)
    out_shape = [jax.ShapeDtypeStruct((1024, ALL_WIDE), jnp.bfloat16)]
    operands = [own, *weights, cosines, sines]
    in_specs = [vmem, anywhere, anywhere, anywhere, vmem, vmem]
    if exchange:
        out_shape.append(jax.ShapeDtypeStruct((1024, HEADS_WIDE), jnp.bfloat16))
        operands.append(grad)
        in_specs.append(vmem)
    return pl.pallas_call(
        functools.partial(gather_kernel, exchange),
        out_shape=out_shape,
        in_specs=in_specs,
        out_specs=[vmem] * len(out_shape),
        scratch_shapes=[
            pltpu.VMEM((1024, COLS), jnp.bfloat16),
            pltpu.VMEM((COLS, ALL_WIDE), jnp.bfloat16),
            pltpu.SemaphoreType.DMA((5,)),
            pltpu.SemaphoreType.DMA((count,)),
            pltpu.SemaphoreType.DMA((count,)),
        ],
        compiler_params=pltpu.CompilerParams(
            collective_id=collective_id, has_side_effects=True
        ),
    )(*operands)


def add_rows(out, terms, count, chunk=256):
    @pl.loop(0, count // chunk)
    def _(step):
        rows = pl.ds(pl.multiple_of(step * chunk, chunk), chunk)
        total = terms[0][rows, :].astype(jnp.float32)
        for term in terms[1:]:
            total = total + term[rows, :].astype(jnp.float32)
        out[rows, :] = total.astype(jnp.bfloat16)


def reduce_kernel(
    turned,
    query_ref,
    key_ref,
    value_ref,
    mixed_ref,
    sum_ref,
    owned_ref,
    weight,
    shares,
    z_in,
    far_right,
    far_left,
    near_right,
    near_left,
    far_right_one,
    far_left_one,
    near_right_one,
    near_left_one,
    z_last,
    local_sems,
    send_sems,
    recv_sems,
):
    me, x, z = place()
    loads = load_weights((query_ref, key_ref, value_ref), weight, local_sems)
    greet([(me + step) % 8 for step in range(1, 8)])
    copies = Copies(send_sems, recv_sems)
    right, left, partner = peer_of(x + 1, z), peer_of(x + 3, z), peer_of(x, 1 - z)

    def owned_cols(peer):
        return owned_ref.at[:, pl.ds(pl.multiple_of(peer * HEADS_WIDE, HEADS_WIDE), HEADS_WIDE)]

    def mixed_rows(peer):
        return mixed_ref.at[pl.ds(pl.multiple_of(peer * ROWS, ROWS), ROWS), :]

    kept = pltpu.make_async_copy(mixed_rows(me), owned_cols(me), local_sems.at[3])
    kept.start()
    for one in loads:
        one.wait()

    def share(xx, zz, offset, count):
        return shares.at[peer_of(xx, zz), pl.ds(offset, count), :]

    def pair_share(xx, offset, count):
        return shares.at[pl.ds(2 * (xx % 4), 2), pl.ds(offset, count), :]

    def compute(delta):
        pair = (x + delta) % 4

        @pl.loop(0, 8)
        def _(step):
            rows = pl.ds(pl.multiple_of(step * 512, 512), 512)
            product = jnp.dot(weight[rows, :], turned[pair], preferred_element_type=jnp.float32)
            shares[2 * pair, rows, :] = product[:, :128].astype(jnp.bfloat16)
            shares[2 * pair + 1, rows, :] = product[:, 128:].astype(jnp.bfloat16)

        copies.send(delta, share(x + delta, 1 - z, 0, 2048), z_in.at[delta], partner)

    compute(2)
    copies.send(5, pair_share(x + 2, 2048, 1024), far_right, right)
    copies.send(11, pair_share(x + 2, 3072, 1024), far_left, left)
    compute(1)
    copies.send(6, pair_share(x + 1, 3072, 1024), near_right.at[:, pl.ds(1024, 1024), :], right)
    compute(3)
    copies.send(12, pair_share(x + 3, 2048, 1024), near_left.at[:, pl.ds(0, 1024), :], left)
    compute(0)
    copies.arrived(5, far_right, left)
    for zz in range(2):
        spot = shares.at[2 * ((x + 1) % 4) + zz, pl.ds(2048, 1024), :]
        add_rows(spot, [spot, far_right.at[zz]], 1024)
    copies.send(7, pair_share(x + 1, 2048, 1024), near_right.at[:, pl.ds(0, 1024), :], right)
    copies.arrived(11, far_left, right)
    for zz in range(2):
        spot = shares.at[2 * ((x + 3) % 4) + zz, pl.ds(3072, 1024), :]
        add_rows(spot, [spot, far_left.at[zz]], 1024)
    copies.send(13, pair_share(x + 3, 3072, 1024), near_left.at[:, pl.ds(1024, 1024), :], left)
    copies.arrived(2, z_in.at[2], partner)
    spot = share(x + 2, z, 0, 2048)
    add_rows(spot, [spot, z_in.at[2]], 2048)
    copies.send(8, share(x + 2, z, 0, 1024), far_right_one, right)
    copies.send(14, share(x + 2, z, 1024, 1024), far_left_one, left)
    for step in range(1, 8):
        peer = (me + step) % 8
        copies.send(16 + step, mixed_rows(peer), owned_cols(me), peer)
    copies.arrived(1, z_in.at[1], partner)
    spot = share(x + 1, z, 1024, 1024)
    add_rows(spot, [spot, z_in.at[1, pl.ds(1024, 1024), :]], 1024)
    copies.send(9, spot, near_right_one.at[pl.ds(1024, 1024), :], right)
    copies.arrived(3, z_in.at[3], partner)
    spot = share(x + 3, z, 0, 1024)
    add_rows(spot, [spot, z_in.at[3, pl.ds(0, 1024), :]], 1024)
    copies.send(15, spot, near_left_one.at[pl.ds(0, 1024), :], left)
    copies.arrived(8, far_right_one, left)
    spot = share(x + 1, z, 0, 1024)
    add_rows(spot, [spot, z_in.at[1, pl.ds(0, 1024), :], far_right_one], 1024)
    copies.send(10, spot, near_right_one.at[pl.ds(0, 1024), :], right)
    copies.arrived(14, far_left_one, right)
    spot = share(x + 3, z, 1024, 1024)
    add_rows(spot, [spot, z_in.at[3, pl.ds(1024, 1024), :], far_left_one], 1024)
    copies.send(16, spot, near_left_one.at[pl.ds(1024, 1024), :], left)
    copies.arrived(6, near_right.at[:, pl.ds(1024, 1024), :], left)
    copies.arrived(12, near_left.at[:, pl.ds(0, 1024), :], right)
    copies.arrived(7, near_right.at[:, pl.ds(0, 1024), :], left)
    copies.arrived(13, near_left.at[:, pl.ds(1024, 1024), :], right)
    spot = share(x, 1 - z, 2048, 2048)
    add_rows(spot, [spot, near_right.at[1 - z], near_left.at[1 - z]], 2048)
    copies.send(4, spot, z_last, partner)

    def total(terms, offset):
        @pl.loop(0, 8)
        def _(step):
            rows = pl.ds(pl.multiple_of(step * 256, 256), 256)
            summed = terms[0][rows, :].astype(jnp.float32)
            for term in terms[1:]:
                summed = summed + term[rows, :].astype(jnp.float32)
            sum_ref[:, pl.ds(pl.multiple_of(offset + step * 256, 256), 256)] = summed.T

    copies.arrived(0, z_in.at[0], partner)
    copies.arrived(9, near_right_one.at[pl.ds(1024, 1024), :], left)
    copies.arrived(15, near_left_one.at[pl.ds(0, 1024), :], right)
    copies.arrived(10, near_right_one.at[pl.ds(0, 1024), :], left)
    copies.arrived(16, near_left_one.at[pl.ds(1024, 1024), :], right)
    total([share(x, z, 0, 2048), z_in.at[0], near_right_one, near_left_one], 0)
    kept.wait()
    for step in range(1, 8):
        peer = (me + 8 - step) % 8
        copies.arrived(16 + step, owned_cols(peer), peer)
    copies.arrived(4, z_last, partner)
    total([share(x, z, 2048, 2048), near_right.at[z], near_left.at[z], z_last], 2048)
    copies.finish()


def reduce_project(turned, weights, mixed, collective_id):
    vmem = pl.BlockSpec(memory_space=pltpu.VMEM)
    anywhere = pl.BlockSpec(memory_space=pl.ANY)
    bf16 = jnp.bfloat16
    return pl.pallas_call(
        reduce_kernel,
        out_shape=[
            jax.ShapeDtypeStruct((ROWS, COLS), jnp.float32),
            jax.ShapeDtypeStruct((ROWS, COLS), bf16),
        ],
        in_specs=[vmem, anywhere, anywhere, anywhere, vmem],
        out_specs=[vmem, vmem],
        scratch_shapes=[
            pltpu.VMEM((COLS, ALL_WIDE), bf16),
            pltpu.VMEM((8, COLS, ROWS), bf16),
            pltpu.VMEM((4, 2048, ROWS), bf16),
            pltpu.VMEM((2, 1024, ROWS), bf16),
            pltpu.VMEM((2, 1024, ROWS), bf16),
            pltpu.VMEM((2, 2048, ROWS), bf16),
            pltpu.VMEM((2, 2048, ROWS), bf16),
            pltpu.VMEM((1024, ROWS), bf16),
            pltpu.VMEM((1024, ROWS), bf16),
            pltpu.VMEM((2048, ROWS), bf16),
            pltpu.VMEM((2048, ROWS), bf16),
            pltpu.VMEM((2048, ROWS), bf16),
            pltpu.SemaphoreType.DMA((4,)),
            pltpu.SemaphoreType.DMA((24,)),
            pltpu.SemaphoreType.DMA((24,)),
        ],
        compiler_params=pltpu.CompilerParams(
            collective_id=collective_id, has_side_effects=True
        ),
    )(turned, *weights, mixed)


def body(
    forward_rows,
    saved_rows,
    output_grad,
    forward_docs,
    backward_docs,
    norm_gain,
    query_weight,
    key_matrix,
    value_matrix,
):
    section_index = lax.axis_index("section")
    first_docs = lax.dynamic_index_in_dim(forward_docs, section_index, 0, keepdims=False)
    back_docs = lax.dynamic_index_in_dim(backward_docs, section_index, 0, keepdims=False)
    gain_row = norm_gain[0]
    weights = (query_weight[0], key_matrix[0], value_matrix[0])
    forward_hidden = forward_rows[0].astype(jnp.float32)
    forward_normed = (forward_hidden * token_scale(forward_hidden) * gain_row).astype(jnp.bfloat16)
    back_hidden = saved_rows[0].astype(jnp.float32)
    back_scale = token_scale(back_hidden)
    back_normed = (back_hidden * back_scale * gain_row).astype(jnp.bfloat16)
    cosines, sines = rotation_tables(jnp.arange(8 * ROWS, dtype=jnp.float32))
    cos_wide = jnp.concatenate([cosines, cosines], 1)
    sin_wide = jnp.concatenate([-sines, sines], 1)
    (forward_heads,) = gather_project(forward_normed, weights, cos_wide, sin_wide, 0)
    mixed_rows = attend(
        forward_heads[:, :512], forward_heads[:, 512:640], forward_heads[:, 640:], first_docs
    )
    back_heads, head_gradients = gather_project(
        back_normed, weights, cos_wide, sin_wide, 1, output_grad[0]
    )
    query_grad, key_grad, value_grad = attend_back(
        back_heads[:, :512],
        back_heads[:, 512:640],
        back_heads[:, 640:],
        head_gradients,
        back_docs,
        cosines,
        sines,
    )
    turned = (
        jnp.concatenate([query_grad, key_grad, value_grad], 1)
        .reshape(4, 256, ALL_WIDE)
        .transpose(0, 2, 1)
    )
    input_sum, owned_rows = reduce_project(turned, weights, mixed_rows, 2)
    first_out = (forward_hidden + owned_rows.astype(jnp.float32)).astype(jnp.bfloat16)
    section_output = passed_along(first_out, "section", 1)
    gained = gain_row * input_sum
    inner_sum = jnp.sum(back_hidden * gained, axis=-1, keepdims=True)
    norm_part = (
        back_scale * gained
        - back_hidden * (back_scale * back_scale * back_scale) * inner_sum / MODEL_WIDTH
    )
    first_grad = (output_grad[0].astype(jnp.float32) + norm_part).astype(jnp.bfloat16)
    input_grad = passed_along(first_grad, "section", -1)
    return (section_output[None], input_grad[None])


def solution(mesh):
    placed = (
        P("section", "seq", None),
        P("section", "seq", None),
        P("section", "seq", None),
        P(),
        P(),
        P("section", None),
        P("section", None, "seq"),
        P("section", None, "seq"),
        P("section", None, "seq"),
    )
    return jax.shard_map(
        body,
        mesh=mesh,
        in_specs=placed,
        out_specs=(P("section", "seq", None), P("section", "seq", None)),
        check_vma=False,
    )
```

```python
import functools

import jax
import jax.numpy as jnp
from jax import lax
from jax.experimental import pallas as pl
from jax.experimental.pallas import tpu as pltpu
from jax.sharding import PartitionSpec as P

MESH = pl.DeviceIdType.MESH
ROWS = 128
COLS = 4096
HEADS_WIDE = 512
ALL_WIDE = 768

MODEL_WIDTH = 4096
HEAD_SIZE = 128


epsilon = 1e-05
rope_base = 500000.0


def passed_along(shard, axis, by):
    peers = lax.axis_size(axis)
    pairs = [(i, i + by) for i in range(peers) if 0 <= i + by < peers]
    return lax.ppermute(shard, axis, pairs)


def rotation_tables(positions):
    half = HEAD_SIZE // 2
    freqs = rope_base ** (-(jnp.arange(half, dtype=jnp.float32) * 2.0 / HEAD_SIZE))
    angles = positions[:, None] * freqs[None, :]
    return (jnp.cos(angles), jnp.sin(angles))


def window(block):
    begin = max(0, block * 256 - 512)
    return begin, (block + 1) * 256 - begin


def set_bias(block, docs_col, docs_row, bias):
    begin, count = window(block)
    shape = (count, 256)
    keys = begin + lax.broadcasted_iota(jnp.int32, shape, 0)
    queries = block * 256 + lax.broadcasted_iota(jnp.int32, shape, 1)
    same = docs_col[pl.ds(begin, count), :] == docs_row[:, pl.ds(block * 256, 256)]
    bias[pl.ds(0, count), :] = jnp.where((keys <= queries) & same, 0.0, -1e30)


def across(left, right):
    return lax.dot_general(
        left, right, (((1,), (1,)), ((), ())), preferred_element_type=jnp.float32
    )


def block_probs(query, key, bias):
    scores = across(key, query) * HEAD_SIZE ** (-0.5) + bias
    exp_scores = jnp.exp(scores - jnp.max(scores, axis=0, keepdims=True))
    return exp_scores * (1.0 / jnp.sum(exp_scores, axis=0, keepdims=True))


def head_cols(head):
    return pl.ds(pl.multiple_of(head * HEAD_SIZE, HEAD_SIZE), HEAD_SIZE)


def attend_block(block, heads, docs_col, docs_row, bias, value_turned, mixed):
    begin, count = window(block)
    rows = pl.ds(block * 256, 256)
    set_bias(block, docs_col, docs_row, bias)

    @pl.loop(0, 4)
    def _(head):
        cols = head_cols(head)
        probability = block_probs(
            heads[rows, cols], heads[pl.ds(begin, count), 512:640], bias[pl.ds(0, count), :]
        )
        turned = jnp.dot(
            value_turned[:, pl.ds(begin, count)],
            probability.astype(jnp.bfloat16),
            preferred_element_type=jnp.float32,
        )
        mixed[rows, cols] = turned.T.astype(jnp.bfloat16)


def attend_back_block(
    block, heads, grads, docs_col, docs_row, cos_turned, sin_turned, bias, key_turned, key_grad, value_grad, out
):
    begin, count = window(block)
    rows, keys = pl.ds(block * 256, 256), pl.ds(begin, count)
    set_bias(block, docs_col, docs_row, bias)

    @pl.loop(0, 4)
    def _(head):
        cols = head_cols(head)
        query, grad = heads[rows, cols], grads[rows, cols]
        probability = block_probs(query, heads[keys, 512:640], bias[pl.ds(0, count), :])
        grad_probs = across(heads[keys, 640:768], grad)
        row_delta = jnp.sum(probability * grad_probs, axis=0, keepdims=True)
        grad_scores = (probability * (grad_probs - row_delta)).astype(jnp.bfloat16)
        value_grad[keys, :] += jnp.dot(
            probability.astype(jnp.bfloat16), grad, preferred_element_type=jnp.float32
        )
        key_grad[keys, :] += jnp.dot(grad_scores, query, preferred_element_type=jnp.float32)
        turned = (
            jnp.dot(key_turned[:, keys], grad_scores, preferred_element_type=jnp.float32)
            * HEAD_SIZE ** (-0.5)
        )
        swapped = jnp.concatenate([turned[64:], turned[:64]], 0)
        turned = turned * cos_turned[:, rows] - swapped * sin_turned[:, rows]
        out[block, cols, :] = turned.astype(jnp.bfloat16)


def finish_back(block, cos_ref, sin_ref, key_grad, value_grad, out):
    rows = pl.ds(block * 256, 256)
    keys = key_grad[rows, :] * HEAD_SIZE ** (-0.5)
    keys = keys * cos_ref[rows, :] - pltpu.roll(keys, 64, 1) * sin_ref[rows, :]
    out[block, 512:640, :] = keys.T.astype(jnp.bfloat16)
    out[block, 640:768, :] = value_grad[rows, :].T.astype(jnp.bfloat16)


def token_scale(hidden):
    return lax.rsqrt(jnp.mean(hidden * hidden, axis=-1, keepdims=True) + epsilon)


def place():
    me = lax.axis_index("seq")
    return me, me // 2, me % 2


def peer_of(x, z):
    return 2 * (x % 4) + z


class Copies:
    def __init__(self, send_sems, recv_sems):
        self.send_sems, self.recv_sems = send_sems, recv_sems
        self.sent = []

    def copy(self, number, src, dst, peer):
        return pltpu.make_async_remote_copy(
            src_ref=src,
            dst_ref=dst,
            send_sem=self.send_sems.at[number],
            recv_sem=self.recv_sems.at[number],
            device_id={"seq": peer},
            device_id_type=MESH,
        )

    def send(self, number, src, dst, peer):
        one = self.copy(number, src, dst, peer)
        one.start()
        self.sent.append(one)

    def arrived(self, number, dst, peer):
        self.copy(number, dst, dst, peer).wait_recv()

    def finish(self):
        for one in self.sent:
            one.wait_send()


def greet(peers):
    barrier = pltpu.get_barrier_semaphore()
    for peer in peers:
        pl.semaphore_signal(barrier, inc=1, device_id={"seq": peer}, device_id_type=MESH)
    pl.semaphore_wait(barrier, len(peers))


def load_weights(weight_refs, whole_weight, sems):
    query_ref, key_ref, value_ref = weight_refs
    copies = [
        pltpu.make_async_copy(query_ref, whole_weight.at[:, 0:512], sems.at[0]),
        pltpu.make_async_copy(key_ref, whole_weight.at[:, 512:640], sems.at[1]),
        pltpu.make_async_copy(value_ref, whole_weight.at[:, 640:768], sems.at[2]),
    ]
    for one in copies:
        one.start()
    return copies


def project_rows(pair, whole, weight, cos_ref, sin_ref, out_ref):
    begin = pl.multiple_of(pair * 256, 256)
    rows = pl.ds(begin, 256)

    @pl.loop(0, 3)
    def _(chunk):
        cols = pl.multiple_of(chunk * 256, 256)
        product = jnp.dot(
            whole[rows, :], weight[:, pl.ds(cols, 256)], preferred_element_type=jnp.float32
        )
        cosines, sines = cos_ref[rows, :], sin_ref[rows, :]
        first, second = product[:, :128], product[:, 128:]
        first_turned = first * cosines + pltpu.roll(first, 64, 1) * sines
        second_turned = second * cosines + pltpu.roll(second, 64, 1) * sines
        second_turned = jnp.where(chunk == 2, second, second_turned)
        out_ref[rows, pl.ds(cols, 128)] = first_turned.astype(jnp.bfloat16)
        out_ref[rows, pl.ds(pl.multiple_of(cols + 128, 128), 128)] = second_turned.astype(
            jnp.bfloat16
        )


def gather_plan(copies, own, whole):
    me, x, z = place()
    right, left, partner = peer_of(x + 1, z), peer_of(x + 3, z), peer_of(x, 1 - z)

    def part(xx, zz, offset, count):
        start = pl.multiple_of(peer_of(xx, zz) * ROWS + offset, 32)
        return whole.at[pl.ds(start, count), :]

    def own_part(offset, count):
        return own.at[pl.ds(offset, count), :]

    def send(number, peer, xx, zz, offset, count):
        copies.send(number, part(xx, zz, offset, count), part(xx, zz, offset, count), peer)

    def got(number, peer, xx, zz, offset, count):
        copies.arrived(number, part(xx, zz, offset, count), peer)

    def begin():
        low, high = own_part(0, 64), own_part(64, 64)
        copies.send(0, low, part(x, z, 0, 64), partner)
        copies.send(6, high, part(x, z, 64, 64), right)
        copies.send(12, high, part(x, z, 64, 64), left)
        copies.send(7, low, part(x, z, 0, 64), right)
        copies.send(13, low, part(x, z, 0, 64), left)
        copies.send(1, high, part(x, z, 64, 64), partner)

    def relay_partner():
        got(0, partner, x, 1 - z, 0, 64)
        send(8, right, x, 1 - z, 0, 64)
        send(14, left, x, 1 - z, 0, 64)

    def relay_high():
        got(6, left, x + 3, z, 64, 64)
        send(9, right, x + 3, z, 64, 32)
        send(2, partner, x + 3, z, 64, 64)
        got(12, right, x + 1, z, 64, 64)
        send(15, left, x + 1, z, 96, 32)
        send(3, partner, x + 1, z, 64, 64)

    def relay_low():
        got(7, left, x + 3, z, 0, 64)
        send(10, right, x + 3, z, 0, 32)
        got(13, right, x + 1, z, 0, 64)
        send(16, left, x + 1, z, 32, 32)

    def own_pair():
        got(1, partner, x, 1 - z, 64, 64)

    def relay_far():
        got(9, left, x + 2, z, 64, 32)
        send(4, partner, x + 2, z, 64, 32)
        got(15, right, x + 2, z, 96, 32)
        send(5, partner, x + 2, z, 96, 32)

    def relay_partner_low():
        got(8, left, x + 3, 1 - z, 0, 64)
        send(11, right, x + 3, 1 - z, 0, 32)
        got(14, right, x + 1, 1 - z, 0, 64)
        send(17, left, x + 1, 1 - z, 32, 32)

    def left_pair():
        got(2, partner, x + 3, 1 - z, 64, 64)

    def right_pair():
        got(3, partner, x + 1, 1 - z, 64, 64)

    def far_pair():
        got(10, left, x + 2, z, 0, 32)
        got(16, right, x + 2, z, 32, 32)
        got(11, left, x + 2, 1 - z, 0, 32)
        got(17, right, x + 2, 1 - z, 32, 32)
        got(4, partner, x + 2, 1 - z, 64, 32)
        got(5, partner, x + 2, 1 - z, 96, 32)

    return (
        begin,
        relay_partner,
        relay_high,
        relay_low,
        own_pair,
        relay_far,
        relay_partner_low,
        left_pair,
        right_pair,
        far_pair,
    )


GATHER_COPIES = 18


def gather_kernel(exchange, *refs):
    own, query_ref, key_ref, value_ref, cos_ref, sin_ref = refs[:6]
    refs = refs[6:]
    if exchange:
        grad_ref, out_ref, heads_ref, whole, weight, local_sems, send_sems, recv_sems = refs
        blocks = [lambda: None] * 4
    else:
        back_heads, back_grads, docs_col, docs_row, cos_turned, sin_turned = refs[:6]
        out_ref, back_out, whole, weight, local_sems, send_sems, recv_sems = refs[6:13]
        bias, key_turned, key_grad, value_grad = refs[13:]

        def back(block):
            attend_back_block(
                block,
                back_heads,
                back_grads,
                docs_col,
                docs_row,
                cos_turned,
                sin_turned,
                bias,
                key_turned,
                key_grad,
                value_grad,
                back_out,
            )

        def first_block():
            key_turned[...] = back_heads[:, 512:640].astype(jnp.float32).T.astype(jnp.bfloat16)
            key_grad[...] = jnp.zeros_like(key_grad)
            value_grad[...] = jnp.zeros_like(value_grad)
            back(0)

        def last_block():
            back(3)
            for block in range(4):
                finish_back(block, cos_ref, sin_ref, key_grad, value_grad, back_out)

        blocks = [first_block, lambda: back(1), lambda: back(2), last_block]
    me, x, z = place()
    loads = load_weights((query_ref, key_ref, value_ref), weight, local_sems)
    mine = pltpu.make_async_copy(
        own, whole.at[pl.ds(pl.multiple_of(me * ROWS, ROWS), ROWS), :], local_sems.at[3]
    )
    mine.start()
    if exchange:
        peers = [(me + step) % 8 for step in range(1, 8)]
    else:
        peers = [peer_of(x + 1, z), peer_of(x + 3, z), peer_of(x, 1 - z)]
    greet(peers)
    copies = Copies(send_sems, recv_sems)
    (
        begin,
        relay_partner,
        relay_high,
        relay_low,
        own_pair,
        relay_far,
        relay_partner_low,
        left_pair,
        right_pair,
        far_pair,
    ) = gather_plan(copies, own, whole)
    begin()

    def heads_rows(peer):
        return heads_ref.at[pl.ds(pl.multiple_of(peer * ROWS, ROWS), ROWS), :]

    def grad_cols(peer):
        return grad_ref.at[:, pl.ds(pl.multiple_of(peer * HEADS_WIDE, HEADS_WIDE), HEADS_WIDE)]

    if exchange:
        kept = pltpu.make_async_copy(grad_cols(me), heads_rows(me), local_sems.at[4])
        kept.start()
    blocks[0]()
    blocks[1]()
    relay_partner()
    relay_high()
    blocks[2]()
    relay_low()
    if exchange:
        for step in range(1, 8):
            peer = (me + step) % 8
            copies.send(GATHER_COPIES + step - 1, grad_cols(peer), heads_rows(me), peer)
    for one in loads:
        one.wait()
    mine.wait()
    own_pair()
    project_rows(x, whole, weight, cos_ref, sin_ref, out_ref)
    relay_partner_low()
    blocks[3]()
    relay_far()
    left_pair()
    project_rows((x + 3) % 4, whole, weight, cos_ref, sin_ref, out_ref)
    right_pair()
    project_rows((x + 1) % 4, whole, weight, cos_ref, sin_ref, out_ref)
    far_pair()
    project_rows((x + 2) % 4, whole, weight, cos_ref, sin_ref, out_ref)
    if exchange:
        kept.wait()
        for step in range(1, 8):
            peer = (me + 8 - step) % 8
            copies.arrived(GATHER_COPIES + step - 1, heads_rows(peer), peer)
    copies.finish()


def gather_project(own, weights, cosines, sines, collective_id, grad=None, back=()):
    exchange = grad is not None
    vmem = pl.BlockSpec(memory_space=pltpu.VMEM)
    anywhere = pl.BlockSpec(memory_space=pl.ANY)
    count = GATHER_COPIES + (7 if exchange else 0)
    out_shape = [jax.ShapeDtypeStruct((1024, ALL_WIDE), jnp.bfloat16)]
    operands = [own, *weights, cosines, sines]
    scratch = [
        pltpu.VMEM((1024, COLS), jnp.bfloat16),
        pltpu.VMEM((COLS, ALL_WIDE), jnp.bfloat16),
        pltpu.SemaphoreType.DMA((5,)),
        pltpu.SemaphoreType.DMA((count,)),
        pltpu.SemaphoreType.DMA((count,)),
    ]
    if exchange:
        out_shape.append(jax.ShapeDtypeStruct((1024, HEADS_WIDE), jnp.bfloat16))
        operands.append(grad)
    else:
        out_shape.append(jax.ShapeDtypeStruct((4, ALL_WIDE, 256), jnp.bfloat16))
        operands.extend(back)
        scratch.extend(
            [
                pltpu.VMEM((768, 256), jnp.float32),
                pltpu.VMEM((HEAD_SIZE, 1024), jnp.bfloat16),
                pltpu.VMEM((1024, HEAD_SIZE), jnp.float32),
                pltpu.VMEM((1024, HEAD_SIZE), jnp.float32),
            ]
        )
    in_specs = [vmem] * len(operands)
    in_specs[1:4] = [anywhere] * 3
    return pl.pallas_call(
        functools.partial(gather_kernel, exchange),
        out_shape=out_shape,
        in_specs=in_specs,
        out_specs=[vmem] * len(out_shape),
        scratch_shapes=scratch,
        compiler_params=pltpu.CompilerParams(
            collective_id=collective_id, has_side_effects=True
        ),
    )(*operands)


def add_rows(out, terms, count, chunk=256):
    @pl.loop(0, count // chunk)
    def _(step):
        rows = pl.ds(pl.multiple_of(step * chunk, chunk), chunk)
        total = terms[0][rows, :].astype(jnp.float32)
        for term in terms[1:]:
            total = total + term[rows, :].astype(jnp.float32)
        out[rows, :] = total.astype(jnp.bfloat16)


def reduce_kernel(
    turned,
    query_ref,
    key_ref,
    value_ref,
    heads,
    docs_col,
    docs_row,
    sum_ref,
    owned_ref,
    weight,
    shares,
    z_in,
    far_right,
    far_left,
    near_right,
    near_left,
    far_right_one,
    far_left_one,
    near_right_one,
    near_left_one,
    z_last,
    bias,
    value_turned,
    mixed_ref,
    local_sems,
    send_sems,
    recv_sems,
):
    me, x, z = place()
    loads = load_weights((query_ref, key_ref, value_ref), weight, local_sems)
    greet([(me + step) % 8 for step in range(1, 8)])
    copies = Copies(send_sems, recv_sems)
    right, left, partner = peer_of(x + 1, z), peer_of(x + 3, z), peer_of(x, 1 - z)

    def owned_cols(peer):
        return owned_ref.at[:, pl.ds(pl.multiple_of(peer * HEADS_WIDE, HEADS_WIDE), HEADS_WIDE)]

    def mixed_rows(peer):
        return mixed_ref.at[pl.ds(pl.multiple_of(peer * ROWS, ROWS), ROWS), :]

    for one in loads:
        one.wait()

    def attend(block):
        attend_block(block, heads, docs_col, docs_row, bias, value_turned, mixed_ref)

    def share(xx, zz, offset, count):
        return shares.at[peer_of(xx, zz), pl.ds(offset, count), :]

    def pair_share(xx, offset, count):
        return shares.at[pl.ds(2 * (xx % 4), 2), pl.ds(offset, count), :]

    def compute(delta):
        pair = (x + delta) % 4

        @pl.loop(0, 8)
        def _(step):
            rows = pl.ds(pl.multiple_of(step * 512, 512), 512)
            product = jnp.dot(weight[rows, :], turned[pair], preferred_element_type=jnp.float32)
            shares[2 * pair, rows, :] = product[:, :128].astype(jnp.bfloat16)
            shares[2 * pair + 1, rows, :] = product[:, 128:].astype(jnp.bfloat16)

        copies.send(delta, share(x + delta, 1 - z, 0, 2048), z_in.at[delta], partner)

    compute(2)
    copies.send(5, pair_share(x + 2, 2048, 1024), far_right, right)
    copies.send(11, pair_share(x + 2, 3072, 1024), far_left, left)
    compute(1)
    copies.send(6, pair_share(x + 1, 3072, 1024), near_right.at[:, pl.ds(1024, 1024), :], right)
    compute(3)
    copies.send(12, pair_share(x + 3, 2048, 1024), near_left.at[:, pl.ds(0, 1024), :], left)
    value_turned[...] = heads[:, 640:768].astype(jnp.float32).T.astype(jnp.bfloat16)
    attend(0)
    copies.arrived(5, far_right, left)
    for zz in range(2):
        spot = shares.at[2 * ((x + 1) % 4) + zz, pl.ds(2048, 1024), :]
        add_rows(spot, [spot, far_right.at[zz]], 1024)
    copies.send(7, pair_share(x + 1, 2048, 1024), near_right.at[:, pl.ds(0, 1024), :], right)
    copies.arrived(11, far_left, right)
    for zz in range(2):
        spot = shares.at[2 * ((x + 3) % 4) + zz, pl.ds(3072, 1024), :]
        add_rows(spot, [spot, far_left.at[zz]], 1024)
    copies.send(13, pair_share(x + 3, 3072, 1024), near_left.at[:, pl.ds(1024, 1024), :], left)
    attend(1)
    compute(0)
    copies.arrived(2, z_in.at[2], partner)
    spot = share(x + 2, z, 0, 2048)
    add_rows(spot, [spot, z_in.at[2]], 2048)
    copies.send(8, share(x + 2, z, 0, 1024), far_right_one, right)
    copies.send(14, share(x + 2, z, 1024, 1024), far_left_one, left)
    attend(2)
    copies.arrived(1, z_in.at[1], partner)
    spot = share(x + 1, z, 1024, 1024)
    add_rows(spot, [spot, z_in.at[1, pl.ds(1024, 1024), :]], 1024)
    copies.send(9, spot, near_right_one.at[pl.ds(1024, 1024), :], right)
    copies.arrived(3, z_in.at[3], partner)
    spot = share(x + 3, z, 0, 1024)
    add_rows(spot, [spot, z_in.at[3, pl.ds(0, 1024), :]], 1024)
    copies.send(15, spot, near_left_one.at[pl.ds(0, 1024), :], left)
    attend(3)
    kept = pltpu.make_async_copy(mixed_rows(me), owned_cols(me), local_sems.at[3])
    kept.start()
    for step in range(1, 8):
        peer = (me + step) % 8
        copies.send(16 + step, mixed_rows(peer), owned_cols(me), peer)
    copies.arrived(8, far_right_one, left)
    spot = share(x + 1, z, 0, 1024)
    add_rows(spot, [spot, z_in.at[1, pl.ds(0, 1024), :], far_right_one], 1024)
    copies.send(10, spot, near_right_one.at[pl.ds(0, 1024), :], right)
    copies.arrived(14, far_left_one, right)
    spot = share(x + 3, z, 1024, 1024)
    add_rows(spot, [spot, z_in.at[3, pl.ds(1024, 1024), :], far_left_one], 1024)
    copies.send(16, spot, near_left_one.at[pl.ds(1024, 1024), :], left)
    copies.arrived(6, near_right.at[:, pl.ds(1024, 1024), :], left)
    copies.arrived(12, near_left.at[:, pl.ds(0, 1024), :], right)
    copies.arrived(7, near_right.at[:, pl.ds(0, 1024), :], left)
    copies.arrived(13, near_left.at[:, pl.ds(1024, 1024), :], right)
    spot = share(x, 1 - z, 2048, 2048)
    add_rows(spot, [spot, near_right.at[1 - z], near_left.at[1 - z]], 2048)
    copies.send(4, spot, z_last, partner)

    def total(terms, offset):
        @pl.loop(0, 8)
        def _(step):
            rows = pl.ds(pl.multiple_of(step * 256, 256), 256)
            summed = terms[0][rows, :].astype(jnp.float32)
            for term in terms[1:]:
                summed = summed + term[rows, :].astype(jnp.float32)
            sum_ref[:, pl.ds(pl.multiple_of(offset + step * 256, 256), 256)] = summed.T

    copies.arrived(0, z_in.at[0], partner)
    copies.arrived(9, near_right_one.at[pl.ds(1024, 1024), :], left)
    copies.arrived(15, near_left_one.at[pl.ds(0, 1024), :], right)
    copies.arrived(10, near_right_one.at[pl.ds(0, 1024), :], left)
    copies.arrived(16, near_left_one.at[pl.ds(1024, 1024), :], right)
    total([share(x, z, 0, 2048), z_in.at[0], near_right_one, near_left_one], 0)
    kept.wait()
    for step in range(1, 8):
        peer = (me + 8 - step) % 8
        copies.arrived(16 + step, owned_cols(peer), peer)
    copies.arrived(4, z_last, partner)
    total([share(x, z, 2048, 2048), near_right.at[z], near_left.at[z], z_last], 2048)
    copies.finish()


def reduce_project(turned, weights, heads, docs, collective_id):
    vmem = pl.BlockSpec(memory_space=pltpu.VMEM)
    anywhere = pl.BlockSpec(memory_space=pl.ANY)
    bf16 = jnp.bfloat16
    return pl.pallas_call(
        reduce_kernel,
        out_shape=[
            jax.ShapeDtypeStruct((ROWS, COLS), jnp.float32),
            jax.ShapeDtypeStruct((ROWS, COLS), bf16),
        ],
        in_specs=[vmem, anywhere, anywhere, anywhere, vmem, vmem, vmem],
        out_specs=[vmem, vmem],
        scratch_shapes=[
            pltpu.VMEM((COLS, ALL_WIDE), bf16),
            pltpu.VMEM((8, COLS, ROWS), bf16),
            pltpu.VMEM((4, 2048, ROWS), bf16),
            pltpu.VMEM((2, 1024, ROWS), bf16),
            pltpu.VMEM((2, 1024, ROWS), bf16),
            pltpu.VMEM((2, 2048, ROWS), bf16),
            pltpu.VMEM((2, 2048, ROWS), bf16),
            pltpu.VMEM((1024, ROWS), bf16),
            pltpu.VMEM((1024, ROWS), bf16),
            pltpu.VMEM((2048, ROWS), bf16),
            pltpu.VMEM((2048, ROWS), bf16),
            pltpu.VMEM((2048, ROWS), bf16),
            pltpu.VMEM((768, 256), jnp.float32),
            pltpu.VMEM((HEAD_SIZE, 1024), bf16),
            pltpu.VMEM((1024, HEADS_WIDE), bf16),
            pltpu.SemaphoreType.DMA((4,)),
            pltpu.SemaphoreType.DMA((24,)),
            pltpu.SemaphoreType.DMA((24,)),
        ],
        compiler_params=pltpu.CompilerParams(
            collective_id=collective_id, has_side_effects=True
        ),
    )(turned, *weights, heads, *docs)


def body(
    forward_rows,
    saved_rows,
    output_grad,
    forward_docs,
    backward_docs,
    norm_gain,
    query_weight,
    key_matrix,
    value_matrix,
):
    section_index = lax.axis_index("section")
    first_docs = lax.dynamic_index_in_dim(forward_docs, section_index, 0, keepdims=False)
    back_docs = lax.dynamic_index_in_dim(backward_docs, section_index, 0, keepdims=False)
    gain_row = norm_gain[0]
    weights = (query_weight[0], key_matrix[0], value_matrix[0])
    forward_hidden = forward_rows[0].astype(jnp.float32)
    forward_normed = (forward_hidden * token_scale(forward_hidden) * gain_row).astype(jnp.bfloat16)
    back_hidden = saved_rows[0].astype(jnp.float32)
    back_scale = token_scale(back_hidden)
    back_normed = (back_hidden * back_scale * gain_row).astype(jnp.bfloat16)
    cosines, sines = rotation_tables(jnp.arange(8 * ROWS, dtype=jnp.float32))
    cos_wide = jnp.concatenate([cosines, cosines], 1)
    sin_wide = jnp.concatenate([-sines, sines], 1)
    back_heads, head_gradients = gather_project(
        back_normed, weights, cos_wide, sin_wide, 1, output_grad[0]
    )
    forward_heads, turned = gather_project(
        forward_normed,
        weights,
        cos_wide,
        sin_wide,
        0,
        None,
        (
            back_heads,
            head_gradients,
            back_docs[:, None],
            back_docs[None, :],
            cos_wide.T,
            sin_wide.T,
        ),
    )
    input_sum, owned_rows = reduce_project(
        turned, weights, forward_heads, (first_docs[:, None], first_docs[None, :]), 2
    )
    first_out = (forward_hidden + owned_rows.astype(jnp.float32)).astype(jnp.bfloat16)
    section_output = passed_along(first_out, "section", 1)
    gained = gain_row * input_sum
    inner_sum = jnp.sum(back_hidden * gained, axis=-1, keepdims=True)
    norm_part = (
        back_scale * gained
        - back_hidden * (back_scale * back_scale * back_scale) * inner_sum / MODEL_WIDTH
    )
    first_grad = (output_grad[0].astype(jnp.float32) + norm_part).astype(jnp.bfloat16)
    input_grad = passed_along(first_grad, "section", -1)
    return (section_output[None], input_grad[None])


def solution(mesh):
    placed = (
        P("section", "seq", None),
        P("section", "seq", None),
        P("section", "seq", None),
        P(),
        P(),
        P("section", None),
        P("section", None, "seq"),
        P("section", None, "seq"),
        P("section", None, "seq"),
    )
    return jax.shard_map(
        body,
        mesh=mesh,
        in_specs=placed,
        out_specs=(P("section", "seq", None), P("section", "seq", None)),
        check_vma=False,
    )
```

```python
import types

import jax
import jax.numpy as jnp
from jax import lax
from jax.experimental import pallas as pl
from jax.experimental.pallas import tpu as pltpu
from jax.sharding import PartitionSpec as P

MESH = pl.DeviceIdType.MESH
ROWS = 128
COLS = 4096
HEADS_WIDE = 512
ALL_WIDE = 768

MODEL_WIDTH = 4096
HEAD_SIZE = 128


epsilon = 1e-05
rope_base = 500000.0


def passed_along(shard, axis, by):
    peers = lax.axis_size(axis)
    pairs = [(i, i + by) for i in range(peers) if 0 <= i + by < peers]
    return lax.ppermute(shard, axis, pairs)


def rotation_tables(positions):
    half = HEAD_SIZE // 2
    freqs = rope_base ** (-(jnp.arange(half, dtype=jnp.float32) * 2.0 / HEAD_SIZE))
    angles = positions[:, None] * freqs[None, :]
    return (jnp.cos(angles), jnp.sin(angles))


def window(block):
    begin = max(0, block * 256 - 512)
    return begin, (block + 1) * 256 - begin


def set_bias(block, docs_col, docs_row, bias):
    begin, count = window(block)
    shape = (count, 256)
    keys = begin + lax.broadcasted_iota(jnp.int32, shape, 0)
    queries = block * 256 + lax.broadcasted_iota(jnp.int32, shape, 1)
    same = docs_col[pl.ds(begin, count), :] == docs_row[:, pl.ds(block * 256, 256)]
    bias[pl.ds(0, count), :] = jnp.where((keys <= queries) & same, 0.0, -1e30)


def across(left, right):
    return lax.dot_general(
        left, right, (((1,), (1,)), ((), ())), preferred_element_type=jnp.float32
    )


def block_probs(query, key, bias):
    scores = across(key, query) * HEAD_SIZE ** (-0.5) + bias
    exp_scores = jnp.exp(scores - jnp.max(scores, axis=0, keepdims=True))
    return exp_scores * (1.0 / jnp.sum(exp_scores, axis=0, keepdims=True))


def head_cols(head):
    return pl.ds(pl.multiple_of(head * HEAD_SIZE, HEAD_SIZE), HEAD_SIZE)


def attend_block(block, heads, docs_col, docs_row, bias, value_turned, mixed):
    begin, count = window(block)
    rows = pl.ds(block * 256, 256)
    set_bias(block, docs_col, docs_row, bias)

    @pl.loop(0, 4)
    def _(head):
        cols = head_cols(head)
        probability = block_probs(
            heads[rows, cols], heads[pl.ds(begin, count), 512:640], bias[pl.ds(0, count), :]
        )
        turned = jnp.dot(
            value_turned[:, pl.ds(begin, count)],
            probability.astype(jnp.bfloat16),
            preferred_element_type=jnp.float32,
        )
        mixed[rows, cols] = turned.T.astype(jnp.bfloat16)


def attend_back_block(
    block, heads, grads, docs_col, docs_row, cos_turned, sin_turned, bias, key_turned, key_grad, value_grad, out
):
    begin, count = window(block)
    rows, keys = pl.ds(block * 256, 256), pl.ds(begin, count)
    set_bias(block, docs_col, docs_row, bias)

    @pl.loop(0, 4)
    def _(head):
        cols = head_cols(head)
        query, grad = heads[rows, cols], grads[rows, cols]
        probability = block_probs(query, heads[keys, 512:640], bias[pl.ds(0, count), :])
        grad_probs = across(heads[keys, 640:768], grad)
        row_delta = jnp.sum(probability * grad_probs, axis=0, keepdims=True)
        grad_scores = (probability * (grad_probs - row_delta)).astype(jnp.bfloat16)
        value_grad[keys, :] += jnp.dot(
            probability.astype(jnp.bfloat16), grad, preferred_element_type=jnp.float32
        )
        key_grad[keys, :] += jnp.dot(grad_scores, query, preferred_element_type=jnp.float32)
        turned = (
            jnp.dot(key_turned[:, keys], grad_scores, preferred_element_type=jnp.float32)
            * HEAD_SIZE ** (-0.5)
        )
        swapped = jnp.concatenate([turned[64:], turned[:64]], 0)
        turned = turned * cos_turned[:, rows] - swapped * sin_turned[:, rows]
        out[block, cols, :] = turned.astype(jnp.bfloat16)


def finish_back(block, cos_ref, sin_ref, key_grad, value_grad, out):
    rows = pl.ds(block * 256, 256)
    keys = key_grad[rows, :] * HEAD_SIZE ** (-0.5)
    keys = keys * cos_ref[rows, :] - pltpu.roll(keys, 64, 1) * sin_ref[rows, :]
    out[block, 512:640, :] = keys.T.astype(jnp.bfloat16)
    out[block, 640:768, :] = value_grad[rows, :].T.astype(jnp.bfloat16)


def token_scale(hidden):
    return lax.rsqrt(jnp.mean(hidden * hidden, axis=-1, keepdims=True) + epsilon)


def place():
    me = lax.axis_index("seq")
    return me, me // 2, me % 2


def peer_of(x, z):
    return 2 * (x % 4) + z


class Copies:
    def __init__(self, send_sems, recv_sems, base):
        self.send_sems, self.recv_sems, self.base = send_sems, recv_sems, base
        self.sent = []

    def copy(self, number, src, dst, peer):
        return pltpu.make_async_remote_copy(
            src_ref=src,
            dst_ref=dst,
            send_sem=self.send_sems.at[self.base + number],
            recv_sem=self.recv_sems.at[self.base + number],
            device_id={"seq": peer},
            device_id_type=MESH,
        )

    def send(self, number, src, dst, peer):
        one = self.copy(number, src, dst, peer)
        one.start()
        self.sent.append(one)

    def arrived(self, number, dst, peer):
        self.copy(number, dst, dst, peer).wait_recv()

    def finish(self):
        for one in self.sent:
            one.wait_send()


def greet(peers):
    barrier = pltpu.get_barrier_semaphore()
    for peer in peers:
        pl.semaphore_signal(barrier, inc=1, device_id={"seq": peer}, device_id_type=MESH)
    pl.semaphore_wait(barrier, len(peers))


def load_weights(weight_refs, whole_weight, sems):
    query_ref, key_ref, value_ref = weight_refs
    copies = [
        pltpu.make_async_copy(query_ref, whole_weight.at[:, 0:512], sems.at[0]),
        pltpu.make_async_copy(key_ref, whole_weight.at[:, 512:640], sems.at[1]),
        pltpu.make_async_copy(value_ref, whole_weight.at[:, 640:768], sems.at[2]),
    ]
    for one in copies:
        one.start()
    return copies


def project_rows(pair, whole, weight, cos_ref, sin_ref, out_ref):
    begin = pl.multiple_of(pair * 256, 256)
    rows = pl.ds(begin, 256)

    @pl.loop(0, 3)
    def _(chunk):
        cols = pl.multiple_of(chunk * 256, 256)
        product = jnp.dot(
            whole[rows, :], weight[:, pl.ds(cols, 256)], preferred_element_type=jnp.float32
        )
        cosines, sines = cos_ref[rows, :], sin_ref[rows, :]
        first, second = product[:, :128], product[:, 128:]
        first_turned = first * cosines + pltpu.roll(first, 64, 1) * sines
        second_turned = second * cosines + pltpu.roll(second, 64, 1) * sines
        second_turned = jnp.where(chunk == 2, second, second_turned)
        out_ref[rows, pl.ds(cols, 128)] = first_turned.astype(jnp.bfloat16)
        out_ref[rows, pl.ds(pl.multiple_of(cols + 128, 128), 128)] = second_turned.astype(
            jnp.bfloat16
        )


def gather_steps(copies, own, whole):
    me, x, z = place()
    right, left, partner = peer_of(x + 1, z), peer_of(x + 3, z), peer_of(x, 1 - z)

    def part(xx, zz, offset, count):
        start = pl.multiple_of(peer_of(xx, zz) * ROWS + offset, 32)
        return whole.at[pl.ds(start, count), :]

    def own_part(offset, count):
        return own.at[pl.ds(offset, count), :]

    def send(number, peer, xx, zz, offset, count):
        copies.send(number, part(xx, zz, offset, count), part(xx, zz, offset, count), peer)

    def got(number, peer, xx, zz, offset, count):
        copies.arrived(number, part(xx, zz, offset, count), peer)

    def begin():
        low, high = own_part(0, 64), own_part(64, 64)
        copies.send(0, low, part(x, z, 0, 64), partner)
        copies.send(6, high, part(x, z, 64, 64), right)
        copies.send(12, high, part(x, z, 64, 64), left)
        copies.send(7, low, part(x, z, 0, 64), right)
        copies.send(13, low, part(x, z, 0, 64), left)
        copies.send(1, high, part(x, z, 64, 64), partner)

    def relay_partner():
        got(0, partner, x, 1 - z, 0, 64)
        send(8, right, x, 1 - z, 0, 64)
        send(14, left, x, 1 - z, 0, 64)

    def relay_high():
        got(6, left, x + 3, z, 64, 64)
        send(9, right, x + 3, z, 64, 32)
        send(2, partner, x + 3, z, 64, 64)
        got(12, right, x + 1, z, 64, 64)
        send(15, left, x + 1, z, 96, 32)
        send(3, partner, x + 1, z, 64, 64)

    def relay_low():
        got(7, left, x + 3, z, 0, 64)
        send(10, right, x + 3, z, 0, 32)
        got(13, right, x + 1, z, 0, 64)
        send(16, left, x + 1, z, 32, 32)

    def own_pair():
        got(1, partner, x, 1 - z, 64, 64)

    def relay_far():
        got(9, left, x + 2, z, 64, 32)
        send(4, partner, x + 2, z, 64, 32)
        got(15, right, x + 2, z, 96, 32)
        send(5, partner, x + 2, z, 96, 32)

    def relay_partner_low():
        got(8, left, x + 3, 1 - z, 0, 64)
        send(11, right, x + 3, 1 - z, 0, 32)
        got(14, right, x + 1, 1 - z, 0, 64)
        send(17, left, x + 1, 1 - z, 32, 32)

    def left_pair():
        got(2, partner, x + 3, 1 - z, 64, 64)

    def right_pair():
        got(3, partner, x + 1, 1 - z, 64, 64)

    def far_pair():
        got(10, left, x + 2, z, 0, 32)
        got(16, right, x + 2, z, 32, 32)
        got(11, left, x + 2, 1 - z, 0, 32)
        got(17, right, x + 2, 1 - z, 32, 32)
        got(4, partner, x + 2, 1 - z, 64, 32)
        got(5, partner, x + 2, 1 - z, 96, 32)

    return types.SimpleNamespace(
        begin=begin,
        relay_partner=relay_partner,
        relay_high=relay_high,
        relay_low=relay_low,
        own_pair=own_pair,
        relay_far=relay_far,
        relay_partner_low=relay_partner_low,
        left_pair=left_pair,
        right_pair=right_pair,
        far_pair=far_pair,
    )


def add_rows(out, terms, count, chunk=256):
    @pl.loop(0, count // chunk)
    def _(step):
        rows = pl.ds(pl.multiple_of(step * chunk, chunk), chunk)
        total = terms[0][rows, :].astype(jnp.float32)
        for term in terms[1:]:
            total = total + term[rows, :].astype(jnp.float32)
        out[rows, :] = total.astype(jnp.bfloat16)


def tick_kernel(
    own_back,
    own_forward,
    grad_ref,
    query_ref,
    key_ref,
    value_ref,
    cos_ref,
    sin_ref,
    cos_turned,
    sin_turned,
    back_col,
    back_row,
    forward_col,
    forward_row,
    sum_ref,
    owned_ref,
    whole_back,
    whole_forward,
    weight,
    back_heads,
    heads,
    back_grads,
    turned,
    bias,
    key_turned,
    key_grad,
    value_grad,
    value_turned,
    mixed_ref,
    shares,
    z_in,
    far_right,
    far_left,
    near_right,
    near_left,
    far_right_one,
    far_left_one,
    near_right_one,
    near_left_one,
    z_last,
    local_sems,
    send_sems,
    recv_sems,
):
    me, x, z = place()
    right, left, partner = peer_of(x + 1, z), peer_of(x + 3, z), peer_of(x, 1 - z)
    loads = load_weights((query_ref, key_ref, value_ref), weight, local_sems)

    def wide_rows(ref, peer):
        return ref.at[pl.ds(pl.multiple_of(peer * ROWS, ROWS), ROWS), :]

    def wide_cols(ref, peer):
        return ref.at[:, pl.ds(pl.multiple_of(peer * HEADS_WIDE, HEADS_WIDE), HEADS_WIDE)]

    kept = [
        pltpu.make_async_copy(own_back, wide_rows(whole_back, me), local_sems.at[3]),
        pltpu.make_async_copy(own_forward, wide_rows(whole_forward, me), local_sems.at[4]),
        pltpu.make_async_copy(wide_cols(grad_ref, me), wide_rows(back_grads, me), local_sems.at[5]),
    ]
    for one in kept:
        one.start()
    others = [(me + step) % 8 for step in range(1, 8)]
    sources = [(me + 8 - step) % 8 for step in range(1, 8)]
    greet(others)
    back_copies = Copies(send_sems, recv_sems, 0)
    forward_copies = Copies(send_sems, recv_sems, 18)
    grad_copies = Copies(send_sems, recv_sems, 36)
    mixed_copies = Copies(send_sems, recv_sems, 43)
    copies = Copies(send_sems, recv_sems, 50)
    back = gather_steps(back_copies, own_back, whole_back)
    forward = gather_steps(forward_copies, own_forward, whole_forward)

    def project(pair, whole, out):
        project_rows(pair % 4, whole, weight, cos_ref, sin_ref, out)

    back.begin()
    back.relay_partner()
    back.relay_high()
    back.relay_low()
    for number, peer in enumerate(others):
        grad_copies.send(number, wide_cols(grad_ref, peer), wide_rows(back_grads, me), peer)
    for one in loads + kept:
        one.wait()
    back.own_pair()
    project(x, whole_back, back_heads)
    back.relay_partner_low()
    back.relay_far()
    forward.begin()
    back.left_pair()
    project(x + 3, whole_back, back_heads)
    back.right_pair()
    project(x + 1, whole_back, back_heads)
    back.far_pair()
    project(x + 2, whole_back, back_heads)
    for number, peer in enumerate(sources):
        grad_copies.arrived(number, wide_rows(back_grads, peer), peer)

    def back_block(block):
        attend_back_block(
            block,
            back_heads,
            back_grads,
            back_col,
            back_row,
            cos_turned,
            sin_turned,
            bias,
            key_turned,
            key_grad,
            value_grad,
            turned,
        )

    key_turned[...] = back_heads[:, 512:640].astype(jnp.float32).T.astype(jnp.bfloat16)
    key_grad[...] = jnp.zeros_like(key_grad)
    value_grad[...] = jnp.zeros_like(value_grad)
    back_block(0)
    back_block(1)
    forward.relay_partner()
    forward.relay_high()
    back_block(2)
    forward.relay_low()
    back_block(3)
    for block in range(4):
        finish_back(block, cos_ref, sin_ref, key_grad, value_grad, turned)

    def share(xx, zz, offset, count):
        return shares.at[peer_of(xx, zz), pl.ds(offset, count), :]

    def pair_share(xx, offset, count):
        return shares.at[pl.ds(2 * (xx % 4), 2), pl.ds(offset, count), :]

    def compute(delta):
        pair = (x + delta) % 4

        @pl.loop(0, 8)
        def _(step):
            rows = pl.ds(pl.multiple_of(step * 512, 512), 512)
            product = jnp.dot(weight[rows, :], turned[pair], preferred_element_type=jnp.float32)
            shares[2 * pair, rows, :] = product[:, :128].astype(jnp.bfloat16)
            shares[2 * pair + 1, rows, :] = product[:, 128:].astype(jnp.bfloat16)

    def attend(block):
        attend_block(block, heads, forward_col, forward_row, bias, value_turned, mixed_ref)

    compute(2)
    compute(1)
    forward.own_pair()
    forward.relay_partner_low()
    forward.relay_far()

    def send_along_z(delta):
        copies.send(delta, share(x + delta, 1 - z, 0, 2048), z_in.at[delta], partner)

    copies.send(5, pair_share(x + 2, 2048, 1024), far_right, right)
    copies.send(11, pair_share(x + 2, 3072, 1024), far_left, left)
    send_along_z(2)
    copies.send(6, pair_share(x + 1, 3072, 1024), near_right.at[:, pl.ds(1024, 1024), :], right)
    send_along_z(1)
    compute(3)
    copies.send(12, pair_share(x + 3, 2048, 1024), near_left.at[:, pl.ds(0, 1024), :], left)
    send_along_z(3)
    compute(0)
    send_along_z(0)
    project(x, whole_forward, heads)
    forward.left_pair()
    project(x + 3, whole_forward, heads)
    forward.right_pair()
    project(x + 1, whole_forward, heads)
    forward.far_pair()
    project(x + 2, whole_forward, heads)
    value_turned[...] = heads[:, 640:768].astype(jnp.float32).T.astype(jnp.bfloat16)
    attend(0)
    copies.arrived(5, far_right, left)
    for zz in range(2):
        spot = shares.at[2 * ((x + 1) % 4) + zz, pl.ds(2048, 1024), :]
        add_rows(spot, [spot, far_right.at[zz]], 1024)
    copies.send(7, pair_share(x + 1, 2048, 1024), near_right.at[:, pl.ds(0, 1024), :], right)
    copies.arrived(11, far_left, right)
    for zz in range(2):
        spot = shares.at[2 * ((x + 3) % 4) + zz, pl.ds(3072, 1024), :]
        add_rows(spot, [spot, far_left.at[zz]], 1024)
    copies.send(13, pair_share(x + 3, 3072, 1024), near_left.at[:, pl.ds(1024, 1024), :], left)
    attend(1)
    copies.arrived(2, z_in.at[2], partner)
    spot = share(x + 2, z, 0, 2048)
    add_rows(spot, [spot, z_in.at[2]], 2048)
    copies.send(8, share(x + 2, z, 0, 1024), far_right_one, right)
    copies.send(14, share(x + 2, z, 1024, 1024), far_left_one, left)
    attend(2)
    copies.arrived(1, z_in.at[1], partner)
    spot = share(x + 1, z, 1024, 1024)
    add_rows(spot, [spot, z_in.at[1, pl.ds(1024, 1024), :]], 1024)
    copies.send(9, spot, near_right_one.at[pl.ds(1024, 1024), :], right)
    copies.arrived(3, z_in.at[3], partner)
    spot = share(x + 3, z, 0, 1024)
    add_rows(spot, [spot, z_in.at[3, pl.ds(0, 1024), :]], 1024)
    copies.send(15, spot, near_left_one.at[pl.ds(0, 1024), :], left)
    attend(3)
    kept_mixed = pltpu.make_async_copy(
        wide_rows(mixed_ref, me), wide_cols(owned_ref, me), local_sems.at[6]
    )
    kept_mixed.start()
    for number, peer in enumerate(others):
        mixed_copies.send(number, wide_rows(mixed_ref, peer), wide_cols(owned_ref, me), peer)
    copies.arrived(8, far_right_one, left)
    spot = share(x + 1, z, 0, 1024)
    add_rows(spot, [spot, z_in.at[1, pl.ds(0, 1024), :], far_right_one], 1024)
    copies.send(10, spot, near_right_one.at[pl.ds(0, 1024), :], right)
    copies.arrived(14, far_left_one, right)
    spot = share(x + 3, z, 1024, 1024)
    add_rows(spot, [spot, z_in.at[3, pl.ds(1024, 1024), :], far_left_one], 1024)
    copies.send(16, spot, near_left_one.at[pl.ds(1024, 1024), :], left)
    copies.arrived(6, near_right.at[:, pl.ds(1024, 1024), :], left)
    copies.arrived(12, near_left.at[:, pl.ds(0, 1024), :], right)
    copies.arrived(7, near_right.at[:, pl.ds(0, 1024), :], left)
    copies.arrived(13, near_left.at[:, pl.ds(1024, 1024), :], right)
    spot = share(x, 1 - z, 2048, 2048)
    add_rows(spot, [spot, near_right.at[1 - z], near_left.at[1 - z]], 2048)
    copies.send(4, spot, z_last, partner)

    def total(terms, offset):
        @pl.loop(0, 8)
        def _(step):
            rows = pl.ds(pl.multiple_of(step * 256, 256), 256)
            summed = terms[0][rows, :].astype(jnp.float32)
            for term in terms[1:]:
                summed = summed + term[rows, :].astype(jnp.float32)
            sum_ref[:, pl.ds(pl.multiple_of(offset + step * 256, 256), 256)] = summed.T

    copies.arrived(0, z_in.at[0], partner)
    copies.arrived(9, near_right_one.at[pl.ds(1024, 1024), :], left)
    copies.arrived(15, near_left_one.at[pl.ds(0, 1024), :], right)
    copies.arrived(10, near_right_one.at[pl.ds(0, 1024), :], left)
    copies.arrived(16, near_left_one.at[pl.ds(1024, 1024), :], right)
    total([share(x, z, 0, 2048), z_in.at[0], near_right_one, near_left_one], 0)
    kept_mixed.wait()
    for number, peer in enumerate(sources):
        mixed_copies.arrived(number, wide_cols(owned_ref, peer), peer)
    copies.arrived(4, z_last, partner)
    total([share(x, z, 2048, 2048), near_right.at[z], near_left.at[z], z_last], 2048)
    for each in (back_copies, forward_copies, grad_copies, mixed_copies, copies):
        each.finish()


def tick(operands, weights):
    vmem = pl.BlockSpec(memory_space=pltpu.VMEM)
    anywhere = pl.BlockSpec(memory_space=pl.ANY)
    bf16, f32 = jnp.bfloat16, jnp.float32
    all_operands = [*operands[:3], *weights, *operands[3:]]
    in_specs = [vmem] * len(all_operands)
    in_specs[3:6] = [anywhere] * 3
    return pl.pallas_call(
        tick_kernel,
        out_shape=[
            jax.ShapeDtypeStruct((ROWS, COLS), f32),
            jax.ShapeDtypeStruct((ROWS, COLS), bf16),
        ],
        in_specs=in_specs,
        out_specs=[vmem, vmem],
        scratch_shapes=[
            pltpu.VMEM((1024, COLS), bf16),
            pltpu.VMEM((1024, COLS), bf16),
            pltpu.VMEM((COLS, ALL_WIDE), bf16),
            pltpu.VMEM((1024, ALL_WIDE), bf16),
            pltpu.VMEM((1024, ALL_WIDE), bf16),
            pltpu.VMEM((1024, HEADS_WIDE), bf16),
            pltpu.VMEM((4, ALL_WIDE, 256), bf16),
            pltpu.VMEM((768, 256), f32),
            pltpu.VMEM((HEAD_SIZE, 1024), bf16),
            pltpu.VMEM((1024, HEAD_SIZE), f32),
            pltpu.VMEM((1024, HEAD_SIZE), f32),
            pltpu.VMEM((HEAD_SIZE, 1024), bf16),
            pltpu.VMEM((1024, HEADS_WIDE), bf16),
            pltpu.VMEM((8, COLS, ROWS), bf16),
            pltpu.VMEM((4, 2048, ROWS), bf16),
            pltpu.VMEM((2, 1024, ROWS), bf16),
            pltpu.VMEM((2, 1024, ROWS), bf16),
            pltpu.VMEM((2, 2048, ROWS), bf16),
            pltpu.VMEM((2, 2048, ROWS), bf16),
            pltpu.VMEM((1024, ROWS), bf16),
            pltpu.VMEM((1024, ROWS), bf16),
            pltpu.VMEM((2048, ROWS), bf16),
            pltpu.VMEM((2048, ROWS), bf16),
            pltpu.VMEM((2048, ROWS), bf16),
            pltpu.SemaphoreType.DMA((7,)),
            pltpu.SemaphoreType.DMA((67,)),
            pltpu.SemaphoreType.DMA((67,)),
        ],
        compiler_params=pltpu.CompilerParams(
            collective_id=0, has_side_effects=True, vmem_limit_bytes=66000000
        ),
    )(*all_operands)


def body(
    forward_rows,
    saved_rows,
    output_grad,
    forward_docs,
    backward_docs,
    norm_gain,
    query_weight,
    key_matrix,
    value_matrix,
):
    section_index = lax.axis_index("section")
    first_docs = lax.dynamic_index_in_dim(forward_docs, section_index, 0, keepdims=False)
    back_docs = lax.dynamic_index_in_dim(backward_docs, section_index, 0, keepdims=False)
    gain_row = norm_gain[0]
    weights = (query_weight[0], key_matrix[0], value_matrix[0])
    forward_hidden = forward_rows[0].astype(jnp.float32)
    forward_normed = (forward_hidden * token_scale(forward_hidden) * gain_row).astype(jnp.bfloat16)
    back_hidden = saved_rows[0].astype(jnp.float32)
    back_scale = token_scale(back_hidden)
    back_normed = (back_hidden * back_scale * gain_row).astype(jnp.bfloat16)
    cosines, sines = rotation_tables(jnp.arange(8 * ROWS, dtype=jnp.float32))
    cos_wide = jnp.concatenate([cosines, cosines], 1)
    sin_wide = jnp.concatenate([-sines, sines], 1)
    input_sum, owned_rows = tick(
        (
            back_normed,
            forward_normed,
            output_grad[0],
            cos_wide,
            sin_wide,
            cos_wide.T,
            sin_wide.T,
            back_docs[:, None],
            back_docs[None, :],
            first_docs[:, None],
            first_docs[None, :],
        ),
        weights,
    )
    first_out = (forward_hidden + owned_rows.astype(jnp.float32)).astype(jnp.bfloat16)
    section_output = passed_along(first_out, "section", 1)
    gained = gain_row * input_sum
    inner_sum = jnp.sum(back_hidden * gained, axis=-1, keepdims=True)
    norm_part = (
        back_scale * gained
        - back_hidden * (back_scale * back_scale * back_scale) * inner_sum / MODEL_WIDTH
    )
    first_grad = (output_grad[0].astype(jnp.float32) + norm_part).astype(jnp.bfloat16)
    input_grad = passed_along(first_grad, "section", -1)
    return (section_output[None], input_grad[None])


def solution(mesh):
    placed = (
        P("section", "seq", None),
        P("section", "seq", None),
        P("section", "seq", None),
        P(),
        P(),
        P("section", None),
        P("section", None, "seq"),
        P("section", None, "seq"),
        P("section", None, "seq"),
    )
    return jax.shard_map(
        body,
        mesh=mesh,
        in_specs=placed,
        out_specs=(P("section", "seq", None), P("section", "seq", None)),
        check_vma=False,
    )
```

```python
import types

import jax
import jax.numpy as jnp
import numpy as np
from jax import lax
from jax.experimental import pallas as pl
from jax.experimental.pallas import tpu as pltpu
from jax.sharding import PartitionSpec as P

MESH = pl.DeviceIdType.MESH
ROWS = 128
COLS = 4096
HEADS_WIDE = 512
ALL_WIDE = 768

MODEL_WIDTH = 4096
HEAD_SIZE = 128


epsilon = 1e-05
rope_base = 500000.0


def rotation_tables():
    half = HEAD_SIZE // 2
    freqs = rope_base ** (-(np.arange(half) * 2.0 / HEAD_SIZE))
    angles = np.arange(8 * ROWS)[:, None] * freqs[None, :]
    cosines, sines = np.cos(angles), np.sin(angles)
    cos_wide = np.concatenate([cosines, cosines], 1).astype(np.float32)
    sin_wide = np.concatenate([-sines, sines], 1).astype(np.float32)
    return (cos_wide, sin_wide, cos_wide.T.copy(), sin_wide.T.copy())


def window(block):
    begin = max(0, block * 256 - 512)
    return begin, (block + 1) * 256 - begin


def set_bias(block, docs_col, docs_row, bias):
    begin, count = window(block)
    shape = (count, 256)
    keys = begin + lax.broadcasted_iota(jnp.int32, shape, 0)
    queries = block * 256 + lax.broadcasted_iota(jnp.int32, shape, 1)
    same = docs_col[pl.ds(begin, count), 0:1] == docs_row[:, pl.ds(block * 256, 256)]
    bias[pl.ds(0, count), :] = jnp.where((keys <= queries) & same, 0.0, -1e30)


def across(left, right):
    return lax.dot_general(
        left, right, (((1,), (1,)), ((), ())), preferred_element_type=jnp.float32
    )


def block_probs(query, key, bias):
    scores = across(key, query) * HEAD_SIZE ** (-0.5) + bias
    exp_scores = jnp.exp(scores - jnp.max(scores, axis=0, keepdims=True))
    return exp_scores * (1.0 / jnp.sum(exp_scores, axis=0, keepdims=True))


def head_cols(head):
    return pl.ds(pl.multiple_of(head * HEAD_SIZE, HEAD_SIZE), HEAD_SIZE)


def attend_block(block, heads, docs_col, docs_row, bias, value_turned, mixed):
    begin, count = window(block)
    rows = pl.ds(block * 256, 256)
    set_bias(block, docs_col, docs_row, bias)

    @pl.loop(0, 4)
    def _(head):
        cols = head_cols(head)
        probability = block_probs(
            heads[rows, cols], heads[pl.ds(begin, count), 512:640], bias[pl.ds(0, count), :]
        )
        turned = jnp.dot(
            value_turned[:, pl.ds(begin, count)],
            probability.astype(jnp.bfloat16),
            preferred_element_type=jnp.float32,
        )
        mixed[rows, cols] = turned.T.astype(jnp.bfloat16)


def attend_back_block(
    block, heads, grads, docs_col, docs_row, cos_turned, sin_turned, bias, key_turned, key_grad, value_grad, out
):
    begin, count = window(block)
    rows, keys = pl.ds(block * 256, 256), pl.ds(begin, count)
    set_bias(block, docs_col, docs_row, bias)

    @pl.loop(0, 4)
    def _(head):
        cols = head_cols(head)
        query, grad = heads[rows, cols], grads[rows, cols]
        probability = block_probs(query, heads[keys, 512:640], bias[pl.ds(0, count), :])
        grad_probs = across(heads[keys, 640:768], grad)
        row_delta = jnp.sum(probability * grad_probs, axis=0, keepdims=True)
        grad_scores = (probability * (grad_probs - row_delta)).astype(jnp.bfloat16)
        value_grad[keys, :] += jnp.dot(
            probability.astype(jnp.bfloat16), grad, preferred_element_type=jnp.float32
        )
        key_grad[keys, :] += jnp.dot(grad_scores, query, preferred_element_type=jnp.float32)
        turned = (
            jnp.dot(key_turned[:, keys], grad_scores, preferred_element_type=jnp.float32)
            * HEAD_SIZE ** (-0.5)
        )
        swapped = jnp.concatenate([turned[64:], turned[:64]], 0)
        turned = turned * cos_turned[:, rows] - swapped * sin_turned[:, rows]
        out[block, cols, :] = turned.astype(jnp.bfloat16)


def finish_back(block, cos_ref, sin_ref, key_grad, value_grad, out):
    rows = pl.ds(block * 256, 256)
    keys = key_grad[rows, :] * HEAD_SIZE ** (-0.5)
    keys = keys * cos_ref[rows, :] - pltpu.roll(keys, 64, 1) * sin_ref[rows, :]
    out[block, 512:640, :] = keys.T.astype(jnp.bfloat16)
    out[block, 640:768, :] = value_grad[rows, :].T.astype(jnp.bfloat16)


def token_scale(hidden):
    return lax.rsqrt(jnp.mean(hidden * hidden, axis=-1, keepdims=True) + epsilon)


def norm_rows(hidden_ref, gain_ref, whole, first_row):
    @pl.loop(0, ROWS // 16)
    def _(step):
        hidden = hidden_ref[pl.ds(pl.multiple_of(step * 16, 16), 16), :].astype(jnp.float32)
        normed = (hidden * token_scale(hidden) * gain_ref[...]).astype(jnp.bfloat16)
        whole[pl.ds(pl.multiple_of(first_row + step * 16, 16), 16), :] = normed


def residual_rows(hidden_ref, owned):
    @pl.loop(0, ROWS // 16)
    def _(step):
        rows = pl.ds(pl.multiple_of(step * 16, 16), 16)
        owned[rows, :] = (
            hidden_ref[rows, :].astype(jnp.float32) + owned[rows, :].astype(jnp.float32)
        ).astype(jnp.bfloat16)


def gradient_rows(piece, hidden_ref, grad_rows, gain_ref, sum_ref, out):
    @pl.loop(0, 2)
    def _(step):
        rows = pl.ds(pl.multiple_of(piece * 32 + step * 16, 16), 16)
        hidden = hidden_ref[rows, :].astype(jnp.float32)
        scale = token_scale(hidden)
        gained = gain_ref[...] * sum_ref[rows, :]
        inner_sum = jnp.sum(hidden * gained, axis=-1, keepdims=True)
        norm_part = scale * gained - hidden * (scale * scale * scale * inner_sum / MODEL_WIDTH)
        out[rows, :] = (grad_rows[rows, :].astype(jnp.float32) + norm_part).astype(jnp.bfloat16)


def place():
    me = lax.axis_index("seq")
    return me, me // 2, me % 2


def peer_of(x, z):
    return 2 * (x % 4) + z


class Copies:
    def __init__(self, send_sems, recv_sems, base):
        self.send_sems, self.recv_sems, self.base = send_sems, recv_sems, base
        self.sent = []

    def copy(self, number, src, dst, peer):
        return pltpu.make_async_remote_copy(
            src_ref=src,
            dst_ref=dst,
            send_sem=self.send_sems.at[self.base + number],
            recv_sem=self.recv_sems.at[self.base + number],
            device_id=peer if isinstance(peer, dict) else {"seq": peer},
            device_id_type=MESH,
        )

    def send(self, number, src, dst, peer):
        one = self.copy(number, src, dst, peer)
        one.start()
        self.sent.append(one)

    def arrived(self, number, dst, peer):
        self.copy(number, dst, dst, peer).wait_recv()

    def finish(self):
        for one in self.sent:
            one.wait_send()


def greet(peers):
    barrier = pltpu.get_barrier_semaphore()
    for peer in peers:
        device = peer if isinstance(peer, dict) else {"seq": peer}
        pl.semaphore_signal(barrier, inc=1, device_id=device, device_id_type=MESH)
    return barrier


def load_weights(weight_refs, whole_weight, sems):
    query_ref, key_ref, value_ref = weight_refs
    copies = [
        pltpu.make_async_copy(query_ref, whole_weight.at[:, 0:512], sems.at[0]),
        pltpu.make_async_copy(key_ref, whole_weight.at[:, 512:640], sems.at[1]),
        pltpu.make_async_copy(value_ref, whole_weight.at[:, 640:768], sems.at[2]),
    ]
    for one in copies:
        one.start()
    return copies


def project_rows(pair, whole, weight, cos_ref, sin_ref, out_ref):
    begin = pl.multiple_of(pair * 256, 256)
    rows = pl.ds(begin, 256)

    @pl.loop(0, 3)
    def _(chunk):
        cols = pl.multiple_of(chunk * 256, 256)
        product = jnp.dot(
            whole[rows, :], weight[:, pl.ds(cols, 256)], preferred_element_type=jnp.float32
        )
        cosines, sines = cos_ref[rows, :], sin_ref[rows, :]
        first, second = product[:, :128], product[:, 128:]
        first_turned = first * cosines + pltpu.roll(first, 64, 1) * sines
        second_turned = second * cosines + pltpu.roll(second, 64, 1) * sines
        second_turned = jnp.where(chunk == 2, second, second_turned)
        out_ref[rows, pl.ds(cols, 128)] = first_turned.astype(jnp.bfloat16)
        out_ref[rows, pl.ds(pl.multiple_of(cols + 128, 128), 128)] = second_turned.astype(
            jnp.bfloat16
        )


def gather_steps(copies, whole):
    me, x, z = place()
    right, left, partner = peer_of(x + 1, z), peer_of(x + 3, z), peer_of(x, 1 - z)

    def part(xx, zz, offset, count):
        start = pl.multiple_of(peer_of(xx, zz) * ROWS + offset, 32)
        return whole.at[pl.ds(start, count), :]

    def own_part(offset, count):
        return part(x, z, offset, count)

    def send(number, peer, xx, zz, offset, count):
        copies.send(number, part(xx, zz, offset, count), part(xx, zz, offset, count), peer)

    def got(number, peer, xx, zz, offset, count):
        copies.arrived(number, part(xx, zz, offset, count), peer)

    def begin():
        low, high = own_part(0, 64), own_part(64, 64)
        copies.send(0, low, part(x, z, 0, 64), partner)
        copies.send(6, high, part(x, z, 64, 64), right)
        copies.send(12, high, part(x, z, 64, 64), left)
        copies.send(7, low, part(x, z, 0, 64), right)
        copies.send(13, low, part(x, z, 0, 64), left)
        copies.send(1, high, part(x, z, 64, 64), partner)

    def relay_partner():
        got(0, partner, x, 1 - z, 0, 64)
        send(8, right, x, 1 - z, 0, 64)
        send(14, left, x, 1 - z, 0, 64)

    def relay_high():
        got(6, left, x + 3, z, 64, 64)
        send(9, right, x + 3, z, 64, 32)
        send(2, partner, x + 3, z, 64, 64)
        got(12, right, x + 1, z, 64, 64)
        send(15, left, x + 1, z, 96, 32)
        send(3, partner, x + 1, z, 64, 64)

    def relay_low():
        got(7, left, x + 3, z, 0, 64)
        send(10, right, x + 3, z, 0, 32)
        got(13, right, x + 1, z, 0, 64)
        send(16, left, x + 1, z, 32, 32)

    def own_pair():
        got(1, partner, x, 1 - z, 64, 64)

    def relay_far():
        got(9, left, x + 2, z, 64, 32)
        send(4, partner, x + 2, z, 64, 32)
        got(15, right, x + 2, z, 96, 32)
        send(5, partner, x + 2, z, 96, 32)

    def relay_partner_low():
        got(8, left, x + 3, 1 - z, 0, 64)
        send(11, right, x + 3, 1 - z, 0, 32)
        got(14, right, x + 1, 1 - z, 0, 64)
        send(17, left, x + 1, 1 - z, 32, 32)

    def left_pair():
        got(2, partner, x + 3, 1 - z, 64, 64)

    def right_pair():
        got(3, partner, x + 1, 1 - z, 64, 64)

    def far_pair():
        got(10, left, x + 2, z, 0, 32)
        got(16, right, x + 2, z, 32, 32)
        got(11, left, x + 2, 1 - z, 0, 32)
        got(17, right, x + 2, 1 - z, 32, 32)
        got(4, partner, x + 2, 1 - z, 64, 32)
        got(5, partner, x + 2, 1 - z, 96, 32)

    return types.SimpleNamespace(
        begin=begin,
        relay_partner=relay_partner,
        relay_high=relay_high,
        relay_low=relay_low,
        own_pair=own_pair,
        relay_far=relay_far,
        relay_partner_low=relay_partner_low,
        left_pair=left_pair,
        right_pair=right_pair,
        far_pair=far_pair,
    )


def add_rows(out, terms, count, chunk=256):
    @pl.loop(0, count // chunk)
    def _(step):
        rows = pl.ds(pl.multiple_of(step * chunk, chunk), chunk)
        total = terms[0][rows, :].astype(jnp.float32)
        for term in terms[1:]:
            total = total + term[rows, :].astype(jnp.float32)
        out[rows, :] = total.astype(jnp.bfloat16)


def tick_kernel(
    back_hbm,
    forward_hbm,
    grad_hbm,
    query_ref,
    key_ref,
    value_ref,
    cos_hbm,
    sin_hbm,
    cos_turned_hbm,
    sin_turned_hbm,
    gain_ref,
    back_docs,
    forward_docs,
    section_out,
    gradient_out,
    back_hidden,
    forward_hidden,
    grad_ref,
    cos_ref,
    sin_ref,
    cos_turned,
    sin_turned,
    back_col,
    forward_col,
    sum_ref,
    owned_ref,
    gradient,
    whole_back,
    whole_forward,
    weight,
    back_heads,
    heads,
    back_grads,
    turned,
    bias,
    key_turned,
    key_grad,
    value_grad,
    value_turned,
    mixed_ref,
    shares,
    z_in,
    far_right,
    far_left,
    near_right,
    near_left,
    far_right_one,
    far_left_one,
    near_right_one,
    near_left_one,
    z_last,
    local_sems,
    send_sems,
    recv_sems,
):
    me, x, z = place()
    right, left, partner = peer_of(x + 1, z), peer_of(x + 3, z), peer_of(x, 1 - z)
    section = lax.axis_index("section")
    after, before = (section + 1) % 16, (section + 15) % 16
    first_load = pltpu.make_async_copy(back_hbm, back_hidden, local_sems.at[7])
    first_load.start()
    others = [(me + step) % 8 for step in range(1, 8)]
    sources = [(me + 8 - step) % 8 for step in range(1, 8)]
    barrier = greet([*others, {"section": after}, {"section": before}])
    back_row = back_docs[pl.ds(section, 1), :].astype(jnp.float32)
    forward_row = forward_docs[pl.ds(section, 1), :].astype(jnp.float32)

    def wide_rows(ref, peer):
        return ref.at[pl.ds(pl.multiple_of(peer * ROWS, ROWS), ROWS), :]

    def wide_cols(ref, peer):
        return ref.at[:, pl.ds(pl.multiple_of(peer * HEADS_WIDE, HEADS_WIDE), HEADS_WIDE)]

    pairs = [
        (wide_cols(grad_hbm, me), wide_rows(back_grads, me)),
        (cos_hbm, cos_ref),
        (sin_hbm, sin_ref),
        (forward_hbm, forward_hidden),
        (cos_turned_hbm, cos_turned),
        (sin_turned_hbm, sin_turned),
        (grad_hbm, grad_ref),
    ]
    kept = [
        pltpu.make_async_copy(src, dst, local_sems.at[8 + i]) for i, (src, dst) in enumerate(pairs)
    ]
    first_load.wait()
    loads = load_weights((query_ref, key_ref, value_ref), weight, local_sems)
    for one in kept:
        one.start()
    norm_rows(back_hidden, gain_ref, whole_back, me * ROWS)
    pl.semaphore_wait(barrier, 9)
    back_copies = Copies(send_sems, recv_sems, 0)
    forward_copies = Copies(send_sems, recv_sems, 18)
    grad_copies = Copies(send_sems, recv_sems, 36)
    mixed_copies = Copies(send_sems, recv_sems, 43)
    copies = Copies(send_sems, recv_sems, 50)
    section_copies = Copies(send_sems, recv_sems, 67)
    back = gather_steps(back_copies, whole_back)
    forward = gather_steps(forward_copies, whole_forward)

    def project(pair, whole, out):
        project_rows(pair % 4, whole, weight, cos_ref, sin_ref, out)

    back.begin()
    for one in loads + kept:
        one.wait()
    norm_rows(forward_hidden, gain_ref, whole_forward, me * ROWS)
    back_col[...] = jnp.broadcast_to(back_row, (128, 1024)).T
    forward_col[...] = jnp.broadcast_to(forward_row, (128, 1024)).T
    back.relay_partner()
    back.relay_high()
    back.relay_low()
    for number, peer in enumerate(others):
        grad_copies.send(number, wide_cols(grad_ref, peer), wide_rows(back_grads, me), peer)
    back.own_pair()
    project(x, whole_back, back_heads)
    back.relay_partner_low()
    back.relay_far()
    forward.begin()
    back.left_pair()
    project(x + 3, whole_back, back_heads)
    back.right_pair()
    project(x + 1, whole_back, back_heads)
    back.far_pair()
    project(x + 2, whole_back, back_heads)
    for number, peer in enumerate(sources):
        grad_copies.arrived(number, wide_rows(back_grads, peer), peer)

    def back_block(block):
        attend_back_block(
            block,
            back_heads,
            back_grads,
            back_col,
            back_row,
            cos_turned,
            sin_turned,
            bias,
            key_turned,
            key_grad,
            value_grad,
            turned,
        )

    key_turned[...] = back_heads[:, 512:640].astype(jnp.float32).T.astype(jnp.bfloat16)
    key_grad[...] = jnp.zeros_like(key_grad)
    value_grad[...] = jnp.zeros_like(value_grad)
    back_block(0)
    back_block(1)
    forward.relay_partner()
    forward.relay_high()
    back_block(2)
    forward.relay_low()
    back_block(3)
    for block in range(4):
        finish_back(block, cos_ref, sin_ref, key_grad, value_grad, turned)

    def share(xx, zz, offset, count):
        return shares.at[peer_of(xx, zz), pl.ds(offset, count), :]

    def pair_share(xx, offset, count):
        return shares.at[pl.ds(2 * (xx % 4), 2), pl.ds(offset, count), :]

    def compute(delta):
        pair = (x + delta) % 4

        @pl.loop(0, 8)
        def _(step):
            rows = pl.ds(pl.multiple_of(step * 512, 512), 512)
            product = jnp.dot(weight[rows, :], turned[pair], preferred_element_type=jnp.float32)
            shares[2 * pair, rows, :] = product[:, :128].astype(jnp.bfloat16)
            shares[2 * pair + 1, rows, :] = product[:, 128:].astype(jnp.bfloat16)

    def attend(block):
        attend_block(block, heads, forward_col, forward_row, bias, value_turned, mixed_ref)

    compute(2)
    compute(1)
    forward.own_pair()
    forward.relay_partner_low()
    forward.relay_far()

    def send_along_z(delta):
        copies.send(delta, share(x + delta, 1 - z, 0, 2048), z_in.at[delta], partner)

    copies.send(5, pair_share(x + 2, 2048, 1024), far_right, right)
    copies.send(11, pair_share(x + 2, 3072, 1024), far_left, left)
    send_along_z(2)
    copies.send(6, pair_share(x + 1, 3072, 1024), near_right.at[:, pl.ds(1024, 1024), :], right)
    send_along_z(1)
    compute(3)
    copies.send(12, pair_share(x + 3, 2048, 1024), near_left.at[:, pl.ds(0, 1024), :], left)
    send_along_z(3)
    compute(0)
    send_along_z(0)
    project(x, whole_forward, heads)
    forward.left_pair()
    project(x + 3, whole_forward, heads)
    forward.right_pair()
    project(x + 1, whole_forward, heads)
    forward.far_pair()
    project(x + 2, whole_forward, heads)
    value_turned[...] = heads[:, 640:768].astype(jnp.float32).T.astype(jnp.bfloat16)
    attend(0)
    copies.arrived(5, far_right, left)
    for zz in range(2):
        spot = shares.at[2 * ((x + 1) % 4) + zz, pl.ds(2048, 1024), :]
        add_rows(spot, [spot, far_right.at[zz]], 1024)
    copies.send(7, pair_share(x + 1, 2048, 1024), near_right.at[:, pl.ds(0, 1024), :], right)
    copies.arrived(11, far_left, right)
    for zz in range(2):
        spot = shares.at[2 * ((x + 3) % 4) + zz, pl.ds(3072, 1024), :]
        add_rows(spot, [spot, far_left.at[zz]], 1024)
    copies.send(13, pair_share(x + 3, 3072, 1024), near_left.at[:, pl.ds(1024, 1024), :], left)
    attend(1)
    copies.arrived(2, z_in.at[2], partner)
    spot = share(x + 2, z, 0, 2048)
    add_rows(spot, [spot, z_in.at[2]], 2048)
    copies.send(8, share(x + 2, z, 0, 1024), far_right_one, right)
    copies.send(14, share(x + 2, z, 1024, 1024), far_left_one, left)
    attend(2)
    copies.arrived(1, z_in.at[1], partner)
    spot = share(x + 1, z, 1024, 1024)
    add_rows(spot, [spot, z_in.at[1, pl.ds(1024, 1024), :]], 1024)
    copies.send(9, spot, near_right_one.at[pl.ds(1024, 1024), :], right)
    copies.arrived(3, z_in.at[3], partner)
    spot = share(x + 3, z, 0, 1024)
    add_rows(spot, [spot, z_in.at[3, pl.ds(0, 1024), :]], 1024)
    copies.send(15, spot, near_left_one.at[pl.ds(0, 1024), :], left)
    attend(3)
    kept_mixed = pltpu.make_async_copy(
        wide_rows(mixed_ref, me), wide_cols(owned_ref, me), local_sems.at[6]
    )
    kept_mixed.start()
    for number, peer in enumerate(others):
        mixed_copies.send(number, wide_rows(mixed_ref, peer), wide_cols(owned_ref, me), peer)
    copies.arrived(8, far_right_one, left)
    spot = share(x + 1, z, 0, 1024)
    add_rows(spot, [spot, z_in.at[1, pl.ds(0, 1024), :], far_right_one], 1024)
    copies.send(10, spot, near_right_one.at[pl.ds(0, 1024), :], right)
    copies.arrived(14, far_left_one, right)
    spot = share(x + 3, z, 1024, 1024)
    add_rows(spot, [spot, z_in.at[3, pl.ds(1024, 1024), :], far_left_one], 1024)
    copies.send(16, spot, near_left_one.at[pl.ds(1024, 1024), :], left)
    copies.arrived(6, near_right.at[:, pl.ds(1024, 1024), :], left)
    copies.arrived(12, near_left.at[:, pl.ds(0, 1024), :], right)
    copies.arrived(7, near_right.at[:, pl.ds(0, 1024), :], left)
    copies.arrived(13, near_left.at[:, pl.ds(1024, 1024), :], right)
    spot = share(x, 1 - z, 2048, 2048)
    add_rows(spot, [spot, near_right.at[1 - z], near_left.at[1 - z]], 2048)
    copies.send(4, spot, z_last, partner)

    def total(terms, offset):
        @pl.loop(0, 8)
        def _(step):
            rows = pl.ds(pl.multiple_of(step * 256, 256), 256)
            summed = terms[0][rows, :].astype(jnp.float32)
            for term in terms[1:]:
                summed = summed + term[rows, :].astype(jnp.float32)
            sum_ref[:, pl.ds(pl.multiple_of(offset + step * 256, 256), 256)] = summed.T

    copies.arrived(0, z_in.at[0], partner)
    copies.arrived(9, near_right_one.at[pl.ds(1024, 1024), :], left)
    copies.arrived(15, near_left_one.at[pl.ds(0, 1024), :], right)
    copies.arrived(10, near_right_one.at[pl.ds(0, 1024), :], left)
    copies.arrived(16, near_left_one.at[pl.ds(1024, 1024), :], right)
    total([share(x, z, 0, 2048), z_in.at[0], near_right_one, near_left_one], 0)
    kept_mixed.wait()
    for number, peer in enumerate(sources):
        mixed_copies.arrived(number, wide_cols(owned_ref, peer), peer)
    residual_rows(forward_hidden, owned_ref)

    def piece_rows(ref, piece):
        return ref.at[pl.ds(piece * 32, 32), :]

    forward_out = section_copies.copy(0, owned_ref, section_out, {"section": after})

    def gradient_copy(piece, src):
        return section_copies.copy(
            1 + piece, piece_rows(src, piece), piece_rows(gradient_out, piece), {"section": before}
        )

    def send_piece(piece):
        @pl.when(section > 0)
        def _():
            gradient_copy(piece, gradient).start()

    @pl.when(section < 15)
    def _():
        forward_out.start()

    copies.arrived(4, z_last, partner)
    total([share(x, z, 2048, 2048), near_right.at[z], near_left.at[z], z_last], 2048)
    for piece in range(4):
        gradient_rows(piece, back_hidden, grad_ref, gain_ref, sum_ref, gradient)
        if piece > 0:
            send_piece(piece - 1)
    send_piece(3)

    @pl.when(section == 0)
    def _():
        section_out[...] = jnp.zeros_like(section_out)

    @pl.when(section == 15)
    def _():
        gradient_out[...] = jnp.zeros_like(gradient_out)

    for each in (back_copies, forward_copies, grad_copies, mixed_copies, copies):
        each.finish()

    @pl.when(section < 15)
    def _():
        forward_out.wait_send()
        for piece in range(4):
            gradient_copy(piece, gradient_out).wait_recv()

    @pl.when(section > 0)
    def _():
        section_copies.copy(0, section_out, section_out, {"section": before}).wait_recv()
        for piece in range(4):
            gradient_copy(piece, gradient).wait_send()


def tick(operands, weights):
    vmem = pl.BlockSpec(memory_space=pltpu.VMEM)
    anywhere = pl.BlockSpec(memory_space=pl.ANY)
    bf16, f32 = jnp.bfloat16, jnp.float32
    all_operands = [*operands[:3], *weights, *operands[3:]]
    in_specs = [anywhere] * 10 + [vmem] * 3
    return pl.pallas_call(
        tick_kernel,
        out_shape=[
            jax.ShapeDtypeStruct((ROWS, COLS), bf16),
            jax.ShapeDtypeStruct((ROWS, COLS), bf16),
        ],
        in_specs=in_specs,
        out_specs=[vmem, vmem],
        scratch_shapes=[
            pltpu.VMEM((ROWS, COLS), bf16),
            pltpu.VMEM((ROWS, COLS), bf16),
            pltpu.VMEM((ROWS, COLS), bf16),
            pltpu.VMEM((1024, HEAD_SIZE), f32),
            pltpu.VMEM((1024, HEAD_SIZE), f32),
            pltpu.VMEM((HEAD_SIZE, 1024), f32),
            pltpu.VMEM((HEAD_SIZE, 1024), f32),
            pltpu.VMEM((1024, 128), f32),
            pltpu.VMEM((1024, 128), f32),
            pltpu.VMEM((ROWS, COLS), f32),
            pltpu.VMEM((ROWS, COLS), bf16),
            pltpu.VMEM((ROWS, COLS), bf16),
            pltpu.VMEM((1024, COLS), bf16),
            pltpu.VMEM((1024, COLS), bf16),
            pltpu.VMEM((COLS, ALL_WIDE), bf16),
            pltpu.VMEM((1024, ALL_WIDE), bf16),
            pltpu.VMEM((1024, ALL_WIDE), bf16),
            pltpu.VMEM((1024, HEADS_WIDE), bf16),
            pltpu.VMEM((4, ALL_WIDE, 256), bf16),
            pltpu.VMEM((768, 256), f32),
            pltpu.VMEM((HEAD_SIZE, 1024), bf16),
            pltpu.VMEM((1024, HEAD_SIZE), f32),
            pltpu.VMEM((1024, HEAD_SIZE), f32),
            pltpu.VMEM((HEAD_SIZE, 1024), bf16),
            pltpu.VMEM((1024, HEADS_WIDE), bf16),
            pltpu.VMEM((8, COLS, ROWS), bf16),
            pltpu.VMEM((4, 2048, ROWS), bf16),
            pltpu.VMEM((2, 1024, ROWS), bf16),
            pltpu.VMEM((2, 1024, ROWS), bf16),
            pltpu.VMEM((2, 2048, ROWS), bf16),
            pltpu.VMEM((2, 2048, ROWS), bf16),
            pltpu.VMEM((1024, ROWS), bf16),
            pltpu.VMEM((1024, ROWS), bf16),
            pltpu.VMEM((2048, ROWS), bf16),
            pltpu.VMEM((2048, ROWS), bf16),
            pltpu.VMEM((2048, ROWS), bf16),
            pltpu.SemaphoreType.DMA((15,)),
            pltpu.SemaphoreType.DMA((72,)),
            pltpu.SemaphoreType.DMA((72,)),
        ],
        compiler_params=pltpu.CompilerParams(
            collective_id=0, has_side_effects=True, vmem_limit_bytes=66000000
        ),
    )(*all_operands)


def body(
    forward_rows,
    saved_rows,
    output_grad,
    forward_docs,
    backward_docs,
    norm_gain,
    query_weight,
    key_matrix,
    value_matrix,
):
    section_output, input_grad = tick(
        (
            saved_rows[0],
            forward_rows[0],
            output_grad[0],
            *(jnp.asarray(table) for table in rotation_tables()),
            norm_gain,
            backward_docs,
            forward_docs,
        ),
        (query_weight[0], key_matrix[0], value_matrix[0]),
    )
    return (section_output[None], input_grad[None])


def solution(mesh):
    placed = (
        P("section", "seq", None),
        P("section", "seq", None),
        P("section", "seq", None),
        P(),
        P(),
        P("section", None),
        P("section", None, "seq"),
        P("section", None, "seq"),
        P("section", None, "seq"),
    )
    return jax.shard_map(
        body,
        mesh=mesh,
        in_specs=placed,
        out_specs=(P("section", "seq", None), P("section", "seq", None)),
        check_vma=False,
    )
```

```python
import types

import jax
import jax.numpy as jnp
import numpy as np
from jax import lax
from jax.experimental import pallas as pl
from jax.experimental.pallas import tpu as pltpu
from jax.sharding import PartitionSpec as P

MESH = pl.DeviceIdType.MESH
ROWS = 128
COLS = 4096
HEADS_WIDE = 512
ALL_WIDE = 768

MODEL_WIDTH = 4096
HEAD_SIZE = 128


epsilon = 1e-05
rope_base = 500000.0


def rotation_tables():
    half = HEAD_SIZE // 2
    freqs = rope_base ** (-(np.arange(half) * 2.0 / HEAD_SIZE))
    angles = np.arange(8 * ROWS)[:, None] * freqs[None, :]
    cosines, sines = np.cos(angles), np.sin(angles)
    cos_wide = np.concatenate([cosines, cosines], 1).astype(np.float32)
    sin_wide = np.concatenate([-sines, sines], 1).astype(np.float32)
    return (cos_wide, sin_wide, cos_wide.T.copy(), sin_wide.T.copy())


def window(block):
    begin = max(0, block * 256 - 512)
    return begin, (block + 1) * 256 - begin


def set_bias(block, docs_col, docs_row, bias):
    begin, count = window(block)
    shape = (count, 256)
    keys = begin + lax.broadcasted_iota(jnp.int32, shape, 0)
    queries = block * 256 + lax.broadcasted_iota(jnp.int32, shape, 1)
    same = docs_col[pl.ds(begin, count), 0:1] == docs_row[:, pl.ds(block * 256, 256)]
    bias[pl.ds(0, count), :] = jnp.where((keys <= queries) & same, 0.0, -1e30)


def across(left, right):
    return lax.dot_general(
        left, right, (((1,), (1,)), ((), ())), preferred_element_type=jnp.float32
    )


def block_probs(query, key, bias):
    scores = across(key, query) * HEAD_SIZE ** (-0.5) + bias
    exp_scores = jnp.exp(scores - jnp.max(scores, axis=0, keepdims=True))
    return exp_scores * (1.0 / jnp.sum(exp_scores, axis=0, keepdims=True))


def head_cols(head):
    return pl.ds(pl.multiple_of(head * HEAD_SIZE, HEAD_SIZE), HEAD_SIZE)


def attend_block(block, heads, docs_col, docs_row, bias, value_turned, mixed):
    begin, count = window(block)
    rows = pl.ds(block * 256, 256)
    set_bias(block, docs_col, docs_row, bias)

    @pl.loop(0, 4)
    def _(head):
        cols = head_cols(head)
        probability = block_probs(
            heads[rows, cols], heads[pl.ds(begin, count), 512:640], bias[pl.ds(0, count), :]
        )
        turned = jnp.dot(
            value_turned[:, pl.ds(begin, count)],
            probability.astype(jnp.bfloat16),
            preferred_element_type=jnp.float32,
        )
        mixed[rows, cols] = turned.T.astype(jnp.bfloat16)


def attend_back_block(
    block, heads, grads, docs_col, docs_row, cos_turned, sin_turned, bias, key_turned, key_grad, value_grad, out
):
    begin, count = window(block)
    rows, keys = pl.ds(block * 256, 256), pl.ds(begin, count)
    set_bias(block, docs_col, docs_row, bias)

    @pl.loop(0, 4)
    def _(head):
        cols = head_cols(head)
        query, grad = heads[rows, cols], grads[rows, cols]
        probability = block_probs(query, heads[keys, 512:640], bias[pl.ds(0, count), :])
        grad_probs = across(heads[keys, 640:768], grad)
        row_delta = jnp.sum(probability * grad_probs, axis=0, keepdims=True)
        grad_scores = (probability * (grad_probs - row_delta)).astype(jnp.bfloat16)
        value_grad[keys, :] += jnp.dot(
            probability.astype(jnp.bfloat16), grad, preferred_element_type=jnp.float32
        )
        key_grad[keys, :] += jnp.dot(grad_scores, query, preferred_element_type=jnp.float32)
        turned = (
            jnp.dot(key_turned[:, keys], grad_scores, preferred_element_type=jnp.float32)
            * HEAD_SIZE ** (-0.5)
        )
        swapped = jnp.concatenate([turned[64:], turned[:64]], 0)
        turned = turned * cos_turned[:, rows] - swapped * sin_turned[:, rows]
        out[block, cols, :] = turned.astype(jnp.bfloat16)


def finish_back(block, cos_ref, sin_ref, key_grad, value_grad, out):
    rows = pl.ds(block * 256, 256)
    keys = key_grad[rows, :] * HEAD_SIZE ** (-0.5)
    keys = keys * cos_ref[rows, :] - pltpu.roll(keys, 64, 1) * sin_ref[rows, :]
    out[block, 512:640, :] = keys.T.astype(jnp.bfloat16)
    out[block, 640:768, :] = value_grad[rows, :].T.astype(jnp.bfloat16)


def token_scale(hidden):
    return lax.rsqrt(jnp.mean(hidden * hidden, axis=-1, keepdims=True) + epsilon)


def norm_rows(hidden_ref, gain_ref, whole, first_row):
    @pl.loop(0, ROWS // 16)
    def _(step):
        hidden = hidden_ref[pl.ds(pl.multiple_of(step * 16, 16), 16), :].astype(jnp.float32)
        normed = (hidden * token_scale(hidden) * gain_ref[...]).astype(jnp.bfloat16)
        whole[pl.ds(pl.multiple_of(first_row + step * 16, 16), 16), :] = normed


def residual_cols(hidden_ref, owned, peer):
    cols = pl.ds(pl.multiple_of(peer * HEADS_WIDE, HEADS_WIDE), HEADS_WIDE)

    @pl.loop(0, 2)
    def _(step):
        rows = pl.ds(pl.multiple_of(step * 64, 64), 64)
        owned[rows, cols] = (
            hidden_ref[rows, cols].astype(jnp.float32) + owned[rows, cols].astype(jnp.float32)
        ).astype(jnp.bfloat16)


def gradient_rows(piece, hidden_ref, grad_rows, gain_ref, sum_ref, out):
    @pl.loop(0, 2)
    def _(step):
        rows = pl.ds(pl.multiple_of(piece * 32 + step * 16, 16), 16)
        hidden = hidden_ref[rows, :].astype(jnp.float32)
        scale = token_scale(hidden)
        gained = gain_ref[...] * sum_ref[rows, :]
        inner_sum = jnp.sum(hidden * gained, axis=-1, keepdims=True)
        norm_part = scale * gained - hidden * (scale * scale * scale * inner_sum / MODEL_WIDTH)
        out[rows, :] = (grad_rows[rows, :].astype(jnp.float32) + norm_part).astype(jnp.bfloat16)


def place():
    me = lax.axis_index("seq")
    return me, me // 2, me % 2


def peer_of(x, z):
    return 2 * (x % 4) + z


class Copies:
    def __init__(self, send_sems, recv_sems, base):
        self.send_sems, self.recv_sems, self.base = send_sems, recv_sems, base
        self.sent = []

    def copy(self, number, src, dst, peer):
        return pltpu.make_async_remote_copy(
            src_ref=src,
            dst_ref=dst,
            send_sem=self.send_sems.at[self.base + number],
            recv_sem=self.recv_sems.at[self.base + number],
            device_id=peer if isinstance(peer, dict) else {"seq": peer},
            device_id_type=MESH,
        )

    def send(self, number, src, dst, peer):
        one = self.copy(number, src, dst, peer)
        one.start()
        self.sent.append(one)

    def arrived(self, number, dst, peer):
        self.copy(number, dst, dst, peer).wait_recv()

    def finish(self):
        for one in self.sent:
            one.wait_send()


def greet(peers):
    barrier = pltpu.get_barrier_semaphore()
    for peer in peers:
        device = peer if isinstance(peer, dict) else {"seq": peer}
        pl.semaphore_signal(barrier, inc=1, device_id=device, device_id_type=MESH)
    return barrier


def load_weights(weight_refs, whole_weight, sems):
    query_ref, key_ref, value_ref = weight_refs
    copies = [
        pltpu.make_async_copy(query_ref, whole_weight.at[:, 0:512], sems.at[0]),
        pltpu.make_async_copy(key_ref, whole_weight.at[:, 512:640], sems.at[1]),
        pltpu.make_async_copy(value_ref, whole_weight.at[:, 640:768], sems.at[2]),
    ]
    for one in copies:
        one.start()
    return copies


def project_rows(pair, whole, weight, cos_ref, sin_ref, out_ref):
    begin = pl.multiple_of(pair * 256, 256)
    rows = pl.ds(begin, 256)

    @pl.loop(0, 3)
    def _(chunk):
        cols = pl.multiple_of(chunk * 256, 256)
        product = jnp.dot(
            whole[rows, :], weight[:, pl.ds(cols, 256)], preferred_element_type=jnp.float32
        )
        cosines, sines = cos_ref[rows, :], sin_ref[rows, :]
        first, second = product[:, :128], product[:, 128:]
        first_turned = first * cosines + pltpu.roll(first, 64, 1) * sines
        second_turned = second * cosines + pltpu.roll(second, 64, 1) * sines
        second_turned = jnp.where(chunk == 2, second, second_turned)
        out_ref[rows, pl.ds(cols, 128)] = first_turned.astype(jnp.bfloat16)
        out_ref[rows, pl.ds(pl.multiple_of(cols + 128, 128), 128)] = second_turned.astype(
            jnp.bfloat16
        )


def gather_steps(copies, whole):
    me, x, z = place()
    right, left, partner = peer_of(x + 1, z), peer_of(x + 3, z), peer_of(x, 1 - z)

    def part(xx, zz, offset, count):
        start = pl.multiple_of(peer_of(xx, zz) * ROWS + offset, 32)
        return whole.at[pl.ds(start, count), :]

    def own_part(offset, count):
        return part(x, z, offset, count)

    def send(number, peer, xx, zz, offset, count):
        copies.send(number, part(xx, zz, offset, count), part(xx, zz, offset, count), peer)

    def got(number, peer, xx, zz, offset, count):
        copies.arrived(number, part(xx, zz, offset, count), peer)

    def begin():
        low, high = own_part(0, 64), own_part(64, 64)
        copies.send(0, low, part(x, z, 0, 64), partner)
        copies.send(6, high, part(x, z, 64, 64), right)
        copies.send(12, high, part(x, z, 64, 64), left)
        copies.send(7, low, part(x, z, 0, 64), right)
        copies.send(13, low, part(x, z, 0, 64), left)
        copies.send(1, high, part(x, z, 64, 64), partner)

    def relay_partner():
        got(0, partner, x, 1 - z, 0, 64)
        send(8, right, x, 1 - z, 0, 64)
        send(14, left, x, 1 - z, 0, 64)

    def relay_high():
        got(6, left, x + 3, z, 64, 64)
        send(9, right, x + 3, z, 64, 32)
        send(2, partner, x + 3, z, 64, 64)
        got(12, right, x + 1, z, 64, 64)
        send(15, left, x + 1, z, 96, 32)
        send(3, partner, x + 1, z, 64, 64)

    def relay_low():
        got(7, left, x + 3, z, 0, 64)
        send(10, right, x + 3, z, 0, 32)
        got(13, right, x + 1, z, 0, 64)
        send(16, left, x + 1, z, 32, 32)

    def own_pair():
        got(1, partner, x, 1 - z, 64, 64)

    def relay_far():
        got(9, left, x + 2, z, 64, 32)
        send(4, partner, x + 2, z, 64, 32)
        got(15, right, x + 2, z, 96, 32)
        send(5, partner, x + 2, z, 96, 32)

    def relay_partner_low():
        got(8, left, x + 3, 1 - z, 0, 64)
        send(11, right, x + 3, 1 - z, 0, 32)
        got(14, right, x + 1, 1 - z, 0, 64)
        send(17, left, x + 1, 1 - z, 32, 32)

    def left_pair():
        got(2, partner, x + 3, 1 - z, 64, 64)

    def right_pair():
        got(3, partner, x + 1, 1 - z, 64, 64)

    def far_pair():
        got(10, left, x + 2, z, 0, 32)
        got(16, right, x + 2, z, 32, 32)
        got(11, left, x + 2, 1 - z, 0, 32)
        got(17, right, x + 2, 1 - z, 32, 32)
        got(4, partner, x + 2, 1 - z, 64, 32)
        got(5, partner, x + 2, 1 - z, 96, 32)

    return types.SimpleNamespace(
        begin=begin,
        relay_partner=relay_partner,
        relay_high=relay_high,
        relay_low=relay_low,
        own_pair=own_pair,
        relay_far=relay_far,
        relay_partner_low=relay_partner_low,
        left_pair=left_pair,
        right_pair=right_pair,
        far_pair=far_pair,
    )


def add_rows(out, terms, count, chunk=256):
    @pl.loop(0, count // chunk)
    def _(step):
        rows = pl.ds(pl.multiple_of(step * chunk, chunk), chunk)
        total = terms[0][rows, :].astype(jnp.float32)
        for term in terms[1:]:
            total = total + term[rows, :].astype(jnp.float32)
        out[rows, :] = total.astype(jnp.bfloat16)


def tick_kernel(
    back_hbm,
    forward_hbm,
    grad_hbm,
    query_ref,
    key_ref,
    value_ref,
    cos_hbm,
    sin_hbm,
    cos_turned_hbm,
    sin_turned_hbm,
    gain_ref,
    back_docs,
    forward_docs,
    section_out,
    gradient_out,
    back_hidden,
    forward_hidden,
    grad_ref,
    cos_ref,
    sin_ref,
    cos_turned,
    sin_turned,
    back_col,
    forward_col,
    sum_ref,
    owned_ref,
    gradient,
    whole_back,
    whole_forward,
    weight,
    back_heads,
    heads,
    back_grads,
    turned,
    bias,
    key_turned,
    key_grad,
    value_grad,
    value_turned,
    mixed_ref,
    shares,
    z_in,
    far_right,
    far_left,
    near_right,
    near_left,
    far_right_one,
    far_left_one,
    near_right_one,
    near_left_one,
    z_last,
    local_sems,
    send_sems,
    recv_sems,
):
    me, x, z = place()
    right, left, partner = peer_of(x + 1, z), peer_of(x + 3, z), peer_of(x, 1 - z)
    section = lax.axis_index("section")
    after, before = (section + 1) % 16, (section + 15) % 16
    first_load = pltpu.make_async_copy(back_hbm, back_hidden, local_sems.at[7])
    first_load.start()
    others = [(me + step) % 8 for step in range(1, 8)]
    sources = [(me + 8 - step) % 8 for step in range(1, 8)]
    barrier = greet([*others, {"section": after}, {"section": before}])
    back_row = back_docs[pl.ds(section, 1), :].astype(jnp.float32)
    forward_row = forward_docs[pl.ds(section, 1), :].astype(jnp.float32)

    def wide_rows(ref, peer):
        return ref.at[pl.ds(pl.multiple_of(peer * ROWS, ROWS), ROWS), :]

    def wide_cols(ref, peer):
        return ref.at[:, pl.ds(pl.multiple_of(peer * HEADS_WIDE, HEADS_WIDE), HEADS_WIDE)]

    pairs = [
        (wide_cols(grad_hbm, me), wide_rows(back_grads, me)),
        (cos_hbm, cos_ref),
        (sin_hbm, sin_ref),
        (forward_hbm, forward_hidden),
        (cos_turned_hbm, cos_turned),
        (sin_turned_hbm, sin_turned),
        (grad_hbm, grad_ref),
    ]
    kept = [
        pltpu.make_async_copy(src, dst, local_sems.at[8 + i]) for i, (src, dst) in enumerate(pairs)
    ]
    first_load.wait()
    loads = load_weights((query_ref, key_ref, value_ref), weight, local_sems)
    for one in kept:
        one.start()
    norm_rows(back_hidden, gain_ref, whole_back, me * ROWS)
    pl.semaphore_wait(barrier, 9)
    back_copies = Copies(send_sems, recv_sems, 0)
    forward_copies = Copies(send_sems, recv_sems, 18)
    grad_copies = Copies(send_sems, recv_sems, 36)
    mixed_copies = Copies(send_sems, recv_sems, 43)
    copies = Copies(send_sems, recv_sems, 50)
    section_copies = Copies(send_sems, recv_sems, 67)
    back = gather_steps(back_copies, whole_back)
    forward = gather_steps(forward_copies, whole_forward)

    def project(pair, whole, out):
        project_rows(pair % 4, whole, weight, cos_ref, sin_ref, out)

    back.begin()
    for one in loads + kept:
        one.wait()
    norm_rows(forward_hidden, gain_ref, whole_forward, me * ROWS)
    back_col[...] = jnp.broadcast_to(back_row, (128, 1024)).T
    forward_col[...] = jnp.broadcast_to(forward_row, (128, 1024)).T
    back.relay_partner()
    back.relay_high()
    back.relay_low()
    for number, peer in enumerate(others):
        grad_copies.send(number, wide_cols(grad_ref, peer), wide_rows(back_grads, me), peer)
    back.own_pair()
    project(x, whole_back, back_heads)
    back.relay_partner_low()
    back.relay_far()
    forward.begin()
    back.left_pair()
    project(x + 3, whole_back, back_heads)
    back.right_pair()
    project(x + 1, whole_back, back_heads)
    back.far_pair()
    project(x + 2, whole_back, back_heads)
    for number, peer in enumerate(sources):
        grad_copies.arrived(number, wide_rows(back_grads, peer), peer)

    def back_block(block):
        attend_back_block(
            block,
            back_heads,
            back_grads,
            back_col,
            back_row,
            cos_turned,
            sin_turned,
            bias,
            key_turned,
            key_grad,
            value_grad,
            turned,
        )

    key_turned[...] = back_heads[:, 512:640].astype(jnp.float32).T.astype(jnp.bfloat16)
    key_grad[...] = jnp.zeros_like(key_grad)
    value_grad[...] = jnp.zeros_like(value_grad)
    back_block(0)
    back_block(1)
    forward.relay_partner()
    forward.relay_high()
    back_block(2)
    forward.relay_low()
    back_block(3)
    for block in range(4):
        finish_back(block, cos_ref, sin_ref, key_grad, value_grad, turned)

    def share(xx, zz, offset, count):
        return shares.at[peer_of(xx, zz), pl.ds(offset, count), :]

    def pair_share(xx, offset, count):
        return shares.at[pl.ds(2 * (xx % 4), 2), pl.ds(offset, count), :]

    def compute(delta):
        pair = (x + delta) % 4

        @pl.loop(0, 8)
        def _(step):
            rows = pl.ds(pl.multiple_of(step * 512, 512), 512)
            product = jnp.dot(weight[rows, :], turned[pair], preferred_element_type=jnp.float32)
            shares[2 * pair, rows, :] = product[:, :128].astype(jnp.bfloat16)
            shares[2 * pair + 1, rows, :] = product[:, 128:].astype(jnp.bfloat16)

    def attend(block):
        attend_block(block, heads, forward_col, forward_row, bias, value_turned, mixed_ref)

    compute(2)
    compute(1)
    forward.own_pair()
    forward.relay_partner_low()
    forward.relay_far()

    def send_along_z(delta):
        copies.send(delta, share(x + delta, 1 - z, 0, 2048), z_in.at[delta], partner)

    copies.send(5, pair_share(x + 2, 2048, 1024), far_right, right)
    copies.send(11, pair_share(x + 2, 3072, 1024), far_left, left)
    send_along_z(2)
    copies.send(6, pair_share(x + 1, 3072, 1024), near_right.at[:, pl.ds(1024, 1024), :], right)
    send_along_z(1)
    compute(3)
    copies.send(12, pair_share(x + 3, 2048, 1024), near_left.at[:, pl.ds(0, 1024), :], left)
    send_along_z(3)
    compute(0)
    send_along_z(0)
    project(x, whole_forward, heads)
    forward.left_pair()
    project(x + 3, whole_forward, heads)
    forward.right_pair()
    project(x + 1, whole_forward, heads)
    forward.far_pair()
    project(x + 2, whole_forward, heads)
    value_turned[...] = heads[:, 640:768].astype(jnp.float32).T.astype(jnp.bfloat16)
    attend(0)
    copies.arrived(5, far_right, left)
    for zz in range(2):
        spot = shares.at[2 * ((x + 1) % 4) + zz, pl.ds(2048, 1024), :]
        add_rows(spot, [spot, far_right.at[zz]], 1024)
    copies.send(7, pair_share(x + 1, 2048, 1024), near_right.at[:, pl.ds(0, 1024), :], right)
    copies.arrived(11, far_left, right)
    for zz in range(2):
        spot = shares.at[2 * ((x + 3) % 4) + zz, pl.ds(3072, 1024), :]
        add_rows(spot, [spot, far_left.at[zz]], 1024)
    copies.send(13, pair_share(x + 3, 3072, 1024), near_left.at[:, pl.ds(1024, 1024), :], left)
    attend(1)
    copies.arrived(2, z_in.at[2], partner)
    spot = share(x + 2, z, 0, 2048)
    add_rows(spot, [spot, z_in.at[2]], 2048)
    copies.send(8, share(x + 2, z, 0, 1024), far_right_one, right)
    copies.send(14, share(x + 2, z, 1024, 1024), far_left_one, left)
    attend(2)
    copies.arrived(1, z_in.at[1], partner)
    spot = share(x + 1, z, 1024, 1024)
    add_rows(spot, [spot, z_in.at[1, pl.ds(1024, 1024), :]], 1024)
    copies.send(9, spot, near_right_one.at[pl.ds(1024, 1024), :], right)
    copies.arrived(3, z_in.at[3], partner)
    spot = share(x + 3, z, 0, 1024)
    add_rows(spot, [spot, z_in.at[3, pl.ds(0, 1024), :]], 1024)
    copies.send(15, spot, near_left_one.at[pl.ds(0, 1024), :], left)
    attend(3)
    copies.arrived(6, near_right.at[:, pl.ds(1024, 1024), :], left)
    copies.arrived(12, near_left.at[:, pl.ds(0, 1024), :], right)
    copies.arrived(7, near_right.at[:, pl.ds(0, 1024), :], left)
    copies.arrived(13, near_left.at[:, pl.ds(1024, 1024), :], right)
    spot = share(x, 1 - z, 2048, 2048)
    add_rows(spot, [spot, near_right.at[1 - z], near_left.at[1 - z]], 2048)
    copies.send(4, spot, z_last, partner)
    copies.arrived(8, far_right_one, left)
    spot = share(x + 1, z, 0, 1024)
    add_rows(spot, [spot, z_in.at[1, pl.ds(0, 1024), :], far_right_one], 1024)
    copies.send(10, spot, near_right_one.at[pl.ds(0, 1024), :], right)
    copies.arrived(14, far_left_one, right)
    spot = share(x + 3, z, 1024, 1024)
    add_rows(spot, [spot, z_in.at[3, pl.ds(1024, 1024), :], far_left_one], 1024)
    copies.send(16, spot, near_left_one.at[pl.ds(1024, 1024), :], left)
    kept_mixed = pltpu.make_async_copy(
        wide_rows(mixed_ref, me), wide_cols(owned_ref, me), local_sems.at[6]
    )
    kept_mixed.start()
    for number, peer in enumerate(others):
        mixed_copies.send(number, wide_rows(mixed_ref, peer), wide_cols(owned_ref, me), peer)

    def total(terms, offset):
        @pl.loop(0, 8)
        def _(step):
            rows = pl.ds(pl.multiple_of(step * 256, 256), 256)
            summed = terms[0][rows, :].astype(jnp.float32)
            for term in terms[1:]:
                summed = summed + term[rows, :].astype(jnp.float32)
            sum_ref[:, pl.ds(pl.multiple_of(offset + step * 256, 256), 256)] = summed.T

    copies.arrived(0, z_in.at[0], partner)
    copies.arrived(9, near_right_one.at[pl.ds(1024, 1024), :], left)
    copies.arrived(15, near_left_one.at[pl.ds(0, 1024), :], right)
    copies.arrived(10, near_right_one.at[pl.ds(0, 1024), :], left)
    copies.arrived(16, near_left_one.at[pl.ds(1024, 1024), :], right)
    total([share(x, z, 0, 2048), z_in.at[0], near_right_one, near_left_one], 0)

    def piece_rows(ref, piece):
        return ref.at[pl.ds(piece * 32, 32), :]

    def gradient_copy(piece, src):
        return section_copies.copy(
            8 + piece, piece_rows(src, piece), piece_rows(gradient_out, piece), {"section": before}
        )

    def send_piece(piece):
        @pl.when(section > 0)
        def _():
            gradient_copy(piece, gradient).start()

    copies.arrived(4, z_last, partner)
    total([share(x, z, 2048, 2048), near_right.at[z], near_left.at[z], z_last], 2048)
    for piece in range(4):
        gradient_rows(piece, back_hidden, grad_ref, gain_ref, sum_ref, gradient)
        if piece > 0:
            send_piece(piece - 1)
    send_piece(3)

    def forward_copy(number, peer, src, to):
        return section_copies.copy(
            number, wide_cols(src, peer), wide_cols(section_out, peer), {"section": to}
        )

    def start_forward(number, peer):
        @pl.when(section < 15)
        def _():
            forward_copy(number, peer, owned_ref, after).start()

    for number, peer in enumerate([me, *sources]):
        if number == 0:
            kept_mixed.wait()
        else:
            mixed_copies.arrived(number - 1, wide_cols(owned_ref, peer), peer)
        residual_cols(forward_hidden, owned_ref, peer)
        if number > 0:
            start_forward(number - 1, [me, *sources][number - 1])

    @pl.when(section == 0)
    def _():
        section_out[...] = jnp.zeros_like(section_out)

    @pl.when(section == 15)
    def _():
        gradient_out[...] = jnp.zeros_like(gradient_out)

    start_forward(7, sources[6])
    for each in (back_copies, forward_copies, grad_copies, mixed_copies, copies):
        each.finish()

    @pl.when(section < 15)
    def _():
        for number, peer in enumerate([me, *sources]):
            forward_copy(number, peer, owned_ref, after).wait_send()
        for piece in range(4):
            gradient_copy(piece, gradient_out).wait_recv()

    @pl.when(section > 0)
    def _():
        for number, peer in enumerate([me, *sources]):
            forward_copy(number, peer, section_out, before).wait_recv()
        for piece in range(4):
            gradient_copy(piece, gradient).wait_send()


def tick(operands, weights):
    vmem = pl.BlockSpec(memory_space=pltpu.VMEM)
    anywhere = pl.BlockSpec(memory_space=pl.ANY)
    bf16, f32 = jnp.bfloat16, jnp.float32
    all_operands = [*operands[:3], *weights, *operands[3:]]
    in_specs = [anywhere] * 10 + [vmem] * 3
    return pl.pallas_call(
        tick_kernel,
        out_shape=[
            jax.ShapeDtypeStruct((ROWS, COLS), bf16),
            jax.ShapeDtypeStruct((ROWS, COLS), bf16),
        ],
        in_specs=in_specs,
        out_specs=[vmem, vmem],
        scratch_shapes=[
            pltpu.VMEM((ROWS, COLS), bf16),
            pltpu.VMEM((ROWS, COLS), bf16),
            pltpu.VMEM((ROWS, COLS), bf16),
            pltpu.VMEM((1024, HEAD_SIZE), f32),
            pltpu.VMEM((1024, HEAD_SIZE), f32),
            pltpu.VMEM((HEAD_SIZE, 1024), f32),
            pltpu.VMEM((HEAD_SIZE, 1024), f32),
            pltpu.VMEM((1024, 128), f32),
            pltpu.VMEM((1024, 128), f32),
            pltpu.VMEM((ROWS, COLS), f32),
            pltpu.VMEM((ROWS, COLS), bf16),
            pltpu.VMEM((ROWS, COLS), bf16),
            pltpu.VMEM((1024, COLS), bf16),
            pltpu.VMEM((1024, COLS), bf16),
            pltpu.VMEM((COLS, ALL_WIDE), bf16),
            pltpu.VMEM((1024, ALL_WIDE), bf16),
            pltpu.VMEM((1024, ALL_WIDE), bf16),
            pltpu.VMEM((1024, HEADS_WIDE), bf16),
            pltpu.VMEM((4, ALL_WIDE, 256), bf16),
            pltpu.VMEM((768, 256), f32),
            pltpu.VMEM((HEAD_SIZE, 1024), bf16),
            pltpu.VMEM((1024, HEAD_SIZE), f32),
            pltpu.VMEM((1024, HEAD_SIZE), f32),
            pltpu.VMEM((HEAD_SIZE, 1024), bf16),
            pltpu.VMEM((1024, HEADS_WIDE), bf16),
            pltpu.VMEM((8, COLS, ROWS), bf16),
            pltpu.VMEM((4, 2048, ROWS), bf16),
            pltpu.VMEM((2, 1024, ROWS), bf16),
            pltpu.VMEM((2, 1024, ROWS), bf16),
            pltpu.VMEM((2, 2048, ROWS), bf16),
            pltpu.VMEM((2, 2048, ROWS), bf16),
            pltpu.VMEM((1024, ROWS), bf16),
            pltpu.VMEM((1024, ROWS), bf16),
            pltpu.VMEM((2048, ROWS), bf16),
            pltpu.VMEM((2048, ROWS), bf16),
            pltpu.VMEM((2048, ROWS), bf16),
            pltpu.SemaphoreType.DMA((15,)),
            pltpu.SemaphoreType.DMA((79,)),
            pltpu.SemaphoreType.DMA((79,)),
        ],
        compiler_params=pltpu.CompilerParams(
            collective_id=0, has_side_effects=True, vmem_limit_bytes=66000000
        ),
    )(*all_operands)


def body(
    forward_rows,
    saved_rows,
    output_grad,
    forward_docs,
    backward_docs,
    norm_gain,
    query_weight,
    key_matrix,
    value_matrix,
):
    section_output, input_grad = tick(
        (
            saved_rows[0],
            forward_rows[0],
            output_grad[0],
            *(jnp.asarray(table) for table in rotation_tables()),
            norm_gain,
            backward_docs,
            forward_docs,
        ),
        (query_weight[0], key_matrix[0], value_matrix[0]),
    )
    return (section_output[None], input_grad[None])


def solution(mesh):
    placed = (
        P("section", "seq", None),
        P("section", "seq", None),
        P("section", "seq", None),
        P(),
        P(),
        P("section", None),
        P("section", None, "seq"),
        P("section", None, "seq"),
        P("section", None, "seq"),
    )
    return jax.shard_map(
        body,
        mesh=mesh,
        in_specs=placed,
        out_specs=(P("section", "seq", None), P("section", "seq", None)),
        check_vma=False,
    )
```

```python
import types

import jax
import jax.numpy as jnp
import numpy as np
from jax import lax
from jax.experimental import pallas as pl
from jax.experimental.pallas import tpu as pltpu
from jax.sharding import PartitionSpec as P

MESH = pl.DeviceIdType.MESH
ROWS = 128
COLS = 4096
HEADS_WIDE = 512
ALL_WIDE = 768

MODEL_WIDTH = 4096
HEAD_SIZE = 128


epsilon = 1e-05
rope_base = 500000.0


def rotation_tables():
    half = HEAD_SIZE // 2
    freqs = rope_base ** (-(np.arange(half) * 2.0 / HEAD_SIZE))
    angles = np.arange(8 * ROWS)[:, None] * freqs[None, :]
    cosines, sines = np.cos(angles), np.sin(angles)
    cos_wide = np.concatenate([cosines, cosines], 1).astype(np.float32)
    sin_wide = np.concatenate([-sines, sines], 1).astype(np.float32)
    return (cos_wide, sin_wide, cos_wide.T.copy(), sin_wide.T.copy())


def window(block):
    begin = max(0, block * 256 - 512)
    return begin, (block + 1) * 256 - begin


def set_bias(block, docs_col, docs_row, bias):
    begin, count = window(block)
    shape = (count, 256)
    keys = begin + lax.broadcasted_iota(jnp.int32, shape, 0)
    queries = block * 256 + lax.broadcasted_iota(jnp.int32, shape, 1)
    same = docs_col[pl.ds(begin, count), 0:1] == docs_row[:, pl.ds(block * 256, 256)]
    bias[pl.ds(0, count), :] = jnp.where((keys <= queries) & same, 0.0, -1e30)


def across(left, right):
    return lax.dot_general(
        left, right, (((1,), (1,)), ((), ())), preferred_element_type=jnp.float32
    )


def block_probs(query, key, bias):
    scores = across(key, query) * HEAD_SIZE ** (-0.5) + bias
    exp_scores = jnp.exp(scores - jnp.max(scores, axis=0, keepdims=True))
    return exp_scores * (1.0 / jnp.sum(exp_scores, axis=0, keepdims=True))


def head_cols(head):
    return pl.ds(pl.multiple_of(head * HEAD_SIZE, HEAD_SIZE), HEAD_SIZE)


def attend_block(block, heads, docs_col, docs_row, bias, value_turned, mixed):
    begin, count = window(block)
    rows = pl.ds(block * 256, 256)
    set_bias(block, docs_col, docs_row, bias)

    @pl.loop(0, 4)
    def _(head):
        cols = head_cols(head)
        probability = block_probs(
            heads[rows, cols], heads[pl.ds(begin, count), 512:640], bias[pl.ds(0, count), :]
        )
        turned = jnp.dot(
            value_turned[:, pl.ds(begin, count)],
            probability.astype(jnp.bfloat16),
            preferred_element_type=jnp.float32,
        )
        mixed[rows, cols] = turned.T.astype(jnp.bfloat16)


def attend_back_block(
    block, heads, grads, docs_col, docs_row, cos_turned, sin_turned, bias, key_turned, key_grad, value_grad, out
):
    begin, count = window(block)
    rows, keys = pl.ds(block * 256, 256), pl.ds(begin, count)
    set_bias(block, docs_col, docs_row, bias)

    @pl.loop(0, 4)
    def _(head):
        cols = head_cols(head)
        query, grad = heads[rows, cols], grads[rows, cols]
        probability = block_probs(query, heads[keys, 512:640], bias[pl.ds(0, count), :])
        grad_probs = across(heads[keys, 640:768], grad)
        row_delta = jnp.sum(probability * grad_probs, axis=0, keepdims=True)
        grad_scores = (probability * (grad_probs - row_delta)).astype(jnp.bfloat16)
        value_grad[keys, :] += jnp.dot(
            probability.astype(jnp.bfloat16), grad, preferred_element_type=jnp.float32
        )
        key_grad[keys, :] += jnp.dot(grad_scores, query, preferred_element_type=jnp.float32)
        turned = (
            jnp.dot(key_turned[:, keys], grad_scores, preferred_element_type=jnp.float32)
            * HEAD_SIZE ** (-0.5)
        )
        swapped = jnp.concatenate([turned[64:], turned[:64]], 0)
        turned = turned * cos_turned[:, rows] - swapped * sin_turned[:, rows]
        out[block, cols, :] = turned.astype(jnp.bfloat16)


def finish_back(block, cos_ref, sin_ref, key_grad, value_grad, out):
    rows = pl.ds(block * 256, 256)
    keys = key_grad[rows, :] * HEAD_SIZE ** (-0.5)
    keys = keys * cos_ref[rows, :] - pltpu.roll(keys, 64, 1) * sin_ref[rows, :]
    out[block, 512:640, :] = keys.T.astype(jnp.bfloat16)
    out[block, 640:768, :] = value_grad[rows, :].T.astype(jnp.bfloat16)


def token_scale(hidden):
    return lax.rsqrt(jnp.mean(hidden * hidden, axis=-1, keepdims=True) + epsilon)


def norm_rows(hidden_ref, gain_ref, whole, first_row):
    @pl.loop(0, ROWS // 16)
    def _(step):
        hidden = hidden_ref[pl.ds(pl.multiple_of(step * 16, 16), 16), :].astype(jnp.float32)
        normed = (hidden * token_scale(hidden) * gain_ref[...]).astype(jnp.bfloat16)
        whole[pl.ds(pl.multiple_of(first_row + step * 16, 16), 16), :] = normed


def residual_cols(hidden_ref, owned, peer):
    cols = pl.ds(pl.multiple_of(peer * HEADS_WIDE, HEADS_WIDE), HEADS_WIDE)

    @pl.loop(0, 2)
    def _(step):
        rows = pl.ds(pl.multiple_of(step * 64, 64), 64)
        owned[rows, cols] = (
            hidden_ref[rows, cols].astype(jnp.float32) + owned[rows, cols].astype(jnp.float32)
        ).astype(jnp.bfloat16)


def gradient_rows(piece, hidden_ref, grad_rows, gain_ref, sum_ref, out):
    @pl.loop(0, 2)
    def _(step):
        rows = pl.ds(pl.multiple_of(piece * 32 + step * 16, 16), 16)
        hidden = hidden_ref[rows, :].astype(jnp.float32)
        scale = token_scale(hidden)
        gained = gain_ref[...] * sum_ref[rows, :]
        inner_sum = jnp.sum(hidden * gained, axis=-1, keepdims=True)
        norm_part = scale * gained - hidden * (scale * scale * scale * inner_sum / MODEL_WIDTH)
        out[rows, :] = (grad_rows[rows, :].astype(jnp.float32) + norm_part).astype(jnp.bfloat16)


def place():
    me = lax.axis_index("seq")
    return me, me // 2, me % 2


def peer_of(x, z):
    return 2 * (x % 4) + z


class Copies:
    def __init__(self, send_sems, recv_sems, base):
        self.send_sems, self.recv_sems, self.base = send_sems, recv_sems, base
        self.sent = []

    def copy(self, number, src, dst, peer):
        return pltpu.make_async_remote_copy(
            src_ref=src,
            dst_ref=dst,
            send_sem=self.send_sems.at[self.base + number],
            recv_sem=self.recv_sems.at[self.base + number],
            device_id=peer if isinstance(peer, dict) else {"seq": peer},
            device_id_type=MESH,
        )

    def send(self, number, src, dst, peer):
        one = self.copy(number, src, dst, peer)
        one.start()
        self.sent.append(one)

    def arrived(self, number, dst, peer):
        self.copy(number, dst, dst, peer).wait_recv()

    def finish(self):
        for one in self.sent:
            one.wait_send()


def greet(peers):
    barrier = pltpu.get_barrier_semaphore()
    for peer in peers:
        device = peer if isinstance(peer, dict) else {"seq": peer}
        pl.semaphore_signal(barrier, inc=1, device_id=device, device_id_type=MESH)
    return barrier


def load_weights(weight_refs, whole_weight, sems):
    query_ref, key_ref, value_ref = weight_refs
    copies = [
        pltpu.make_async_copy(query_ref, whole_weight.at[:, 0:512], sems.at[0]),
        pltpu.make_async_copy(key_ref, whole_weight.at[:, 512:640], sems.at[1]),
        pltpu.make_async_copy(value_ref, whole_weight.at[:, 640:768], sems.at[2]),
    ]
    for one in copies:
        one.start()
    return copies


def project_rows(pair, whole, weight, cos_ref, sin_ref, out_ref):
    begin = pl.multiple_of(pair * 256, 256)
    rows = pl.ds(begin, 256)

    @pl.loop(0, 3)
    def _(chunk):
        cols = pl.multiple_of(chunk * 256, 256)
        product = jnp.dot(
            whole[rows, :], weight[:, pl.ds(cols, 256)], preferred_element_type=jnp.float32
        )
        cosines, sines = cos_ref[rows, :], sin_ref[rows, :]
        first, second = product[:, :128], product[:, 128:]
        first_turned = first * cosines + pltpu.roll(first, 64, 1) * sines
        second_turned = second * cosines + pltpu.roll(second, 64, 1) * sines
        second_turned = jnp.where(chunk == 2, second, second_turned)
        out_ref[rows, pl.ds(cols, 128)] = first_turned.astype(jnp.bfloat16)
        out_ref[rows, pl.ds(pl.multiple_of(cols + 128, 128), 128)] = second_turned.astype(
            jnp.bfloat16
        )


def gather_steps(copies, whole):
    me, x, z = place()
    right, left, partner = peer_of(x + 1, z), peer_of(x + 3, z), peer_of(x, 1 - z)

    def part(xx, zz, offset, count):
        start = pl.multiple_of(peer_of(xx, zz) * ROWS + offset, 32)
        return whole.at[pl.ds(start, count), :]

    def own_part(offset, count):
        return part(x, z, offset, count)

    def send(number, peer, xx, zz, offset, count):
        copies.send(number, part(xx, zz, offset, count), part(xx, zz, offset, count), peer)

    def got(number, peer, xx, zz, offset, count):
        copies.arrived(number, part(xx, zz, offset, count), peer)

    def begin():
        low, high = own_part(0, 64), own_part(64, 64)
        copies.send(0, low, part(x, z, 0, 64), partner)
        copies.send(6, high, part(x, z, 64, 64), right)
        copies.send(12, high, part(x, z, 64, 64), left)
        copies.send(7, low, part(x, z, 0, 64), right)
        copies.send(13, low, part(x, z, 0, 64), left)
        copies.send(1, high, part(x, z, 64, 64), partner)

    def relay_partner():
        got(0, partner, x, 1 - z, 0, 64)
        send(8, right, x, 1 - z, 0, 64)
        send(14, left, x, 1 - z, 0, 64)

    def relay_high():
        got(6, left, x + 3, z, 64, 64)
        send(9, right, x + 3, z, 64, 32)
        send(2, partner, x + 3, z, 64, 64)
        got(12, right, x + 1, z, 64, 64)
        send(15, left, x + 1, z, 96, 32)
        send(3, partner, x + 1, z, 64, 64)

    def relay_low():
        got(7, left, x + 3, z, 0, 64)
        send(10, right, x + 3, z, 0, 32)
        got(13, right, x + 1, z, 0, 64)
        send(16, left, x + 1, z, 32, 32)

    def own_pair():
        got(1, partner, x, 1 - z, 64, 64)

    def relay_far():
        got(9, left, x + 2, z, 64, 32)
        send(4, partner, x + 2, z, 64, 32)
        got(15, right, x + 2, z, 96, 32)
        send(5, partner, x + 2, z, 96, 32)

    def relay_partner_low():
        got(8, left, x + 3, 1 - z, 0, 64)
        send(11, right, x + 3, 1 - z, 0, 32)
        got(14, right, x + 1, 1 - z, 0, 64)
        send(17, left, x + 1, 1 - z, 32, 32)

    def left_pair():
        got(2, partner, x + 3, 1 - z, 64, 64)

    def right_pair():
        got(3, partner, x + 1, 1 - z, 64, 64)

    def far_pair():
        got(10, left, x + 2, z, 0, 32)
        got(16, right, x + 2, z, 32, 32)
        got(11, left, x + 2, 1 - z, 0, 32)
        got(17, right, x + 2, 1 - z, 32, 32)
        got(4, partner, x + 2, 1 - z, 64, 32)
        got(5, partner, x + 2, 1 - z, 96, 32)

    return types.SimpleNamespace(
        begin=begin,
        relay_partner=relay_partner,
        relay_high=relay_high,
        relay_low=relay_low,
        own_pair=own_pair,
        relay_far=relay_far,
        relay_partner_low=relay_partner_low,
        left_pair=left_pair,
        right_pair=right_pair,
        far_pair=far_pair,
    )


def add_rows(out, terms, count, chunk=256):
    @pl.loop(0, count // chunk)
    def _(step):
        rows = pl.ds(pl.multiple_of(step * chunk, chunk), chunk)
        total = terms[0][rows, :].astype(jnp.float32)
        for term in terms[1:]:
            total = total + term[rows, :].astype(jnp.float32)
        out[rows, :] = total.astype(jnp.bfloat16)


def tick_kernel(
    back_hbm,
    forward_hbm,
    grad_hbm,
    query_ref,
    key_ref,
    value_ref,
    cos_hbm,
    sin_hbm,
    cos_turned_hbm,
    sin_turned_hbm,
    gain_ref,
    back_docs,
    forward_docs,
    section_out,
    gradient_out,
    back_hidden,
    forward_hidden,
    grad_ref,
    cos_ref,
    sin_ref,
    cos_turned,
    sin_turned,
    back_col,
    forward_col,
    sum_ref,
    owned_ref,
    gradient,
    whole_back,
    whole_forward,
    weight,
    back_heads,
    heads,
    back_grads,
    turned,
    bias,
    key_turned,
    key_grad,
    value_grad,
    value_turned,
    mixed_ref,
    shares,
    z_in,
    far_right,
    far_left,
    near_right,
    near_left,
    far_right_one,
    far_left_one,
    near_right_one,
    near_left_one,
    z_last,
    local_sems,
    send_sems,
    recv_sems,
):
    me, x, z = place()
    right, left, partner = peer_of(x + 1, z), peer_of(x + 3, z), peer_of(x, 1 - z)
    section = lax.axis_index("section")
    after, before = (section + 1) % 16, (section + 15) % 16
    first_load = pltpu.make_async_copy(back_hbm, back_hidden, local_sems.at[7])
    first_load.start()
    others = [(me + step) % 8 for step in range(1, 8)]
    sources = [(me + 8 - step) % 8 for step in range(1, 8)]
    barrier = greet([*others, {"section": after}, {"section": before}])
    back_row = back_docs[pl.ds(section, 1), :].astype(jnp.float32)
    forward_row = forward_docs[pl.ds(section, 1), :].astype(jnp.float32)

    def wide_rows(ref, peer):
        return ref.at[pl.ds(pl.multiple_of(peer * ROWS, ROWS), ROWS), :]

    def wide_cols(ref, peer):
        return ref.at[:, pl.ds(pl.multiple_of(peer * HEADS_WIDE, HEADS_WIDE), HEADS_WIDE)]

    pairs = [
        (wide_cols(grad_hbm, me), wide_rows(back_grads, me)),
        (cos_hbm, cos_ref),
        (sin_hbm, sin_ref),
        (forward_hbm, forward_hidden),
        (cos_turned_hbm, cos_turned),
        (sin_turned_hbm, sin_turned),
        (grad_hbm, grad_ref),
    ]
    kept = [
        pltpu.make_async_copy(src, dst, local_sems.at[8 + i]) for i, (src, dst) in enumerate(pairs)
    ]
    first_load.wait()
    loads = load_weights((query_ref, key_ref, value_ref), weight, local_sems)
    for one in kept:
        one.start()
    norm_rows(back_hidden, gain_ref, whole_back, me * ROWS)
    pl.semaphore_wait(barrier, 9)
    back_copies = Copies(send_sems, recv_sems, 0)
    forward_copies = Copies(send_sems, recv_sems, 18)
    grad_copies = Copies(send_sems, recv_sems, 36)
    mixed_copies = Copies(send_sems, recv_sems, 43)
    copies = Copies(send_sems, recv_sems, 50)
    section_copies = Copies(send_sems, recv_sems, 67)
    back = gather_steps(back_copies, whole_back)
    forward = gather_steps(forward_copies, whole_forward)

    def project(pair, whole, out):
        project_rows(pair % 4, whole, weight, cos_ref, sin_ref, out)

    back.begin()
    for one in loads + kept:
        one.wait()
    norm_rows(forward_hidden, gain_ref, whole_forward, me * ROWS)
    back_col[...] = jnp.broadcast_to(back_row, (128, 1024)).T
    forward_col[...] = jnp.broadcast_to(forward_row, (128, 1024)).T
    back.relay_partner()
    back.relay_high()
    back.relay_low()
    for number, peer in enumerate(others):
        grad_copies.send(number, wide_cols(grad_ref, peer), wide_rows(back_grads, me), peer)
    back.own_pair()
    project(x, whole_back, back_heads)
    back.relay_partner_low()
    back.relay_far()
    forward.begin()
    back.left_pair()
    project(x + 3, whole_back, back_heads)
    back.right_pair()
    project(x + 1, whole_back, back_heads)
    back.far_pair()
    project(x + 2, whole_back, back_heads)
    for number, peer in enumerate(sources):
        grad_copies.arrived(number, wide_rows(back_grads, peer), peer)

    def back_block(block):
        attend_back_block(
            block,
            back_heads,
            back_grads,
            back_col,
            back_row,
            cos_turned,
            sin_turned,
            bias,
            key_turned,
            key_grad,
            value_grad,
            turned,
        )

    key_turned[...] = back_heads[:, 512:640].astype(jnp.float32).T.astype(jnp.bfloat16)
    key_grad[...] = jnp.zeros_like(key_grad)
    value_grad[...] = jnp.zeros_like(value_grad)
    back_block(0)
    back_block(1)
    forward.relay_partner()
    forward.relay_high()
    back_block(2)
    forward.relay_low()
    back_block(3)
    for block in range(4):
        finish_back(block, cos_ref, sin_ref, key_grad, value_grad, turned)

    def share(xx, zz, offset, count):
        return shares.at[peer_of(xx, zz), pl.ds(offset, count), :]

    def pair_share(xx, offset, count):
        return shares.at[pl.ds(2 * (xx % 4), 2), pl.ds(offset, count), :]

    def compute(delta):
        pair = (x + delta) % 4

        @pl.loop(0, 8)
        def _(step):
            rows = pl.ds(pl.multiple_of(step * 512, 512), 512)
            product = jnp.dot(weight[rows, :], turned[pair], preferred_element_type=jnp.float32)
            shares[2 * pair, rows, :] = product[:, :128].astype(jnp.bfloat16)
            shares[2 * pair + 1, rows, :] = product[:, 128:].astype(jnp.bfloat16)

    def attend(block):
        attend_block(block, heads, forward_col, forward_row, bias, value_turned, mixed_ref)

    compute(2)
    compute(1)
    forward.own_pair()
    forward.relay_partner_low()
    forward.relay_far()

    def send_along_z(delta):
        copies.send(delta, share(x + delta, 1 - z, 0, 2048), z_in.at[delta], partner)

    copies.send(5, pair_share(x + 2, 2048, 1024), far_right, right)
    copies.send(11, pair_share(x + 2, 3072, 1024), far_left, left)
    send_along_z(2)
    copies.send(6, pair_share(x + 1, 3072, 1024), near_right.at[:, pl.ds(1024, 1024), :], right)
    send_along_z(1)
    compute(3)
    copies.send(12, pair_share(x + 3, 2048, 1024), near_left.at[:, pl.ds(0, 1024), :], left)
    send_along_z(3)
    compute(0)
    send_along_z(0)
    project(x, whole_forward, heads)
    forward.left_pair()
    project(x + 3, whole_forward, heads)
    forward.right_pair()
    project(x + 1, whole_forward, heads)
    forward.far_pair()
    project(x + 2, whole_forward, heads)
    value_turned[...] = heads[:, 640:768].astype(jnp.float32).T.astype(jnp.bfloat16)
    attend(0)
    copies.arrived(5, far_right, left)
    for zz in range(2):
        spot = shares.at[2 * ((x + 1) % 4) + zz, pl.ds(2048, 1024), :]
        add_rows(spot, [spot, far_right.at[zz]], 1024)
    copies.send(7, pair_share(x + 1, 2048, 1024), near_right.at[:, pl.ds(0, 1024), :], right)
    copies.arrived(11, far_left, right)
    for zz in range(2):
        spot = shares.at[2 * ((x + 3) % 4) + zz, pl.ds(3072, 1024), :]
        add_rows(spot, [spot, far_left.at[zz]], 1024)
    copies.send(13, pair_share(x + 3, 3072, 1024), near_left.at[:, pl.ds(1024, 1024), :], left)
    attend(1)
    copies.arrived(2, z_in.at[2], partner)
    spot = share(x + 2, z, 0, 2048)
    add_rows(spot, [spot, z_in.at[2]], 2048)
    copies.send(8, share(x + 2, z, 0, 1024), far_right_one, right)
    copies.send(14, share(x + 2, z, 1024, 1024), far_left_one, left)
    attend(2)
    copies.arrived(1, z_in.at[1], partner)
    spot = share(x + 1, z, 1024, 1024)
    add_rows(spot, [spot, z_in.at[1, pl.ds(1024, 1024), :]], 1024)
    copies.send(9, spot, near_right_one.at[pl.ds(1024, 1024), :], right)
    copies.arrived(3, z_in.at[3], partner)
    spot = share(x + 3, z, 0, 1024)
    add_rows(spot, [spot, z_in.at[3, pl.ds(0, 1024), :]], 1024)
    copies.send(15, spot, near_left_one.at[pl.ds(0, 1024), :], left)
    attend(3)
    copies.arrived(6, near_right.at[:, pl.ds(1024, 1024), :], left)
    copies.arrived(12, near_left.at[:, pl.ds(0, 1024), :], right)
    copies.arrived(7, near_right.at[:, pl.ds(0, 1024), :], left)
    copies.arrived(13, near_left.at[:, pl.ds(1024, 1024), :], right)
    spot = share(x, 1 - z, 2048, 2048)
    add_rows(spot, [spot, near_right.at[1 - z], near_left.at[1 - z]], 2048)
    copies.send(4, spot, z_last, partner)
    copies.arrived(8, far_right_one, left)
    spot = share(x + 1, z, 0, 1024)
    add_rows(spot, [spot, z_in.at[1, pl.ds(0, 1024), :], far_right_one], 1024)
    copies.send(10, spot, near_right_one.at[pl.ds(0, 1024), :], right)
    copies.arrived(14, far_left_one, right)
    spot = share(x + 3, z, 1024, 1024)
    add_rows(spot, [spot, z_in.at[3, pl.ds(1024, 1024), :], far_left_one], 1024)
    copies.send(16, spot, near_left_one.at[pl.ds(1024, 1024), :], left)
    kept_mixed = pltpu.make_async_copy(
        wide_rows(mixed_ref, me), wide_cols(owned_ref, me), local_sems.at[6]
    )
    kept_mixed.start()
    for number, peer in enumerate(others):
        mixed_copies.send(number, wide_rows(mixed_ref, peer), wide_cols(owned_ref, me), peer)

    def total(terms, offset):
        @pl.loop(0, 8)
        def _(step):
            rows = pl.ds(pl.multiple_of(step * 256, 256), 256)
            summed = terms[0][rows, :].astype(jnp.float32)
            for term in terms[1:]:
                summed = summed + term[rows, :].astype(jnp.float32)
            sum_ref[:, pl.ds(pl.multiple_of(offset + step * 256, 256), 256)] = summed.T

    copies.arrived(0, z_in.at[0], partner)
    copies.arrived(9, near_right_one.at[pl.ds(1024, 1024), :], left)
    copies.arrived(15, near_left_one.at[pl.ds(0, 1024), :], right)
    copies.arrived(10, near_right_one.at[pl.ds(0, 1024), :], left)
    copies.arrived(16, near_left_one.at[pl.ds(1024, 1024), :], right)
    total([share(x, z, 0, 2048), z_in.at[0], near_right_one, near_left_one], 0)

    def piece_rows(ref, piece):
        return ref.at[pl.ds(piece * 32, 32), :]

    def gradient_copy(piece, src):
        return section_copies.copy(
            8 + piece, piece_rows(src, piece), piece_rows(gradient_out, piece), {"section": before}
        )

    def send_piece(piece):
        @pl.when(section > 0)
        def _():
            gradient_copy(piece, gradient).start()

    copies.arrived(4, z_last, partner)
    total([share(x, z, 2048, 2048), near_right.at[z], near_left.at[z], z_last], 2048)
    for piece in range(4):
        gradient_rows(piece, back_hidden, grad_ref, gain_ref, sum_ref, gradient)
        if piece > 0:
            send_piece(piece - 1)
    send_piece(3)

    def forward_copy(number, peer, src, to):
        return section_copies.copy(
            number, wide_cols(src, peer), wide_cols(section_out, peer), {"section": to}
        )

    def start_forward(number, peer):
        @pl.when(section < 15)
        def _():
            forward_copy(number, peer, owned_ref, after).start()

    for number, peer in enumerate([me, *sources]):
        if number == 0:
            kept_mixed.wait()
        else:
            mixed_copies.arrived(number - 1, wide_cols(owned_ref, peer), peer)
        residual_cols(forward_hidden, owned_ref, peer)
        if number > 0:
            start_forward(number - 1, [me, *sources][number - 1])

    @pl.when(section == 0)
    def _():
        section_out[...] = jnp.zeros_like(section_out)

    @pl.when(section == 15)
    def _():
        gradient_out[...] = jnp.zeros_like(gradient_out)

    start_forward(7, sources[6])
    for each in (back_copies, forward_copies, grad_copies, mixed_copies, copies):
        each.finish()

    @pl.when(section < 15)
    def _():
        for number, peer in enumerate([me, *sources]):
            forward_copy(number, peer, owned_ref, after).wait_send()
        for piece in range(4):
            gradient_copy(piece, gradient_out).wait_recv()

    @pl.when(section > 0)
    def _():
        for number, peer in enumerate([me, *sources]):
            forward_copy(number, peer, section_out, before).wait_recv()
        for piece in range(4):
            gradient_copy(piece, gradient).wait_send()


def tick(operands, weights):
    vmem = pl.BlockSpec(memory_space=pltpu.VMEM)
    anywhere = pl.BlockSpec(memory_space=pl.ANY)
    bf16, f32 = jnp.bfloat16, jnp.float32
    all_operands = [*operands[:3], *weights, *operands[3:]]
    in_specs = [anywhere] * 10 + [vmem] * 3
    return pl.pallas_call(
        tick_kernel,
        out_shape=[
            jax.ShapeDtypeStruct((ROWS, COLS), bf16),
            jax.ShapeDtypeStruct((ROWS, COLS), bf16),
        ],
        in_specs=in_specs,
        out_specs=[vmem, vmem],
        scratch_shapes=[
            pltpu.VMEM((ROWS, COLS), bf16),
            pltpu.VMEM((ROWS, COLS), bf16),
            pltpu.VMEM((ROWS, COLS), bf16),
            pltpu.VMEM((1024, HEAD_SIZE), f32),
            pltpu.VMEM((1024, HEAD_SIZE), f32),
            pltpu.VMEM((HEAD_SIZE, 1024), f32),
            pltpu.VMEM((HEAD_SIZE, 1024), f32),
            pltpu.VMEM((1024, 128), f32),
            pltpu.VMEM((1024, 128), f32),
            pltpu.VMEM((ROWS, COLS), f32),
            pltpu.VMEM((ROWS, COLS), bf16),
            pltpu.VMEM((ROWS, COLS), bf16),
            pltpu.VMEM((1024, COLS), bf16),
            pltpu.VMEM((1024, COLS), bf16),
            pltpu.VMEM((COLS, ALL_WIDE), bf16),
            pltpu.VMEM((1024, ALL_WIDE), bf16),
            pltpu.VMEM((1024, ALL_WIDE), bf16),
            pltpu.VMEM((1024, HEADS_WIDE), bf16),
            pltpu.VMEM((4, ALL_WIDE, 256), bf16),
            pltpu.VMEM((768, 256), f32),
            pltpu.VMEM((HEAD_SIZE, 1024), bf16),
            pltpu.VMEM((1024, HEAD_SIZE), f32),
            pltpu.VMEM((1024, HEAD_SIZE), f32),
            pltpu.VMEM((HEAD_SIZE, 1024), bf16),
            pltpu.VMEM((1024, HEADS_WIDE), bf16),
            pltpu.VMEM((8, COLS, ROWS), bf16),
            pltpu.VMEM((4, 2048, ROWS), bf16),
            pltpu.VMEM((2, 1024, ROWS), bf16),
            pltpu.VMEM((2, 1024, ROWS), bf16),
            pltpu.VMEM((2, 2048, ROWS), bf16),
            pltpu.VMEM((2, 2048, ROWS), bf16),
            pltpu.VMEM((1024, ROWS), bf16),
            pltpu.VMEM((1024, ROWS), bf16),
            pltpu.VMEM((2048, ROWS), bf16),
            pltpu.VMEM((2048, ROWS), bf16),
            pltpu.VMEM((2048, ROWS), bf16),
            pltpu.SemaphoreType.DMA((15,)),
            pltpu.SemaphoreType.DMA((79,)),
            pltpu.SemaphoreType.DMA((79,)),
        ],
        compiler_params=pltpu.CompilerParams(
            collective_id=0, has_side_effects=True, vmem_limit_bytes=66000000
        ),
    )(*all_operands)


def body(
    forward_rows,
    saved_rows,
    output_grad,
    forward_docs,
    backward_docs,
    norm_gain,
    query_weight,
    key_matrix,
    value_matrix,
):
    section_output, input_grad = tick(
        (
            saved_rows[0],
            forward_rows[0],
            output_grad[0],
            *(jnp.asarray(table) for table in rotation_tables()),
            norm_gain,
            backward_docs,
            forward_docs,
        ),
        (query_weight[0], key_matrix[0], value_matrix[0]),
    )
    section = lax.axis_index("section")
    zero = jnp.zeros((), jnp.bfloat16)
    return (
        jnp.where(section == 0, zero, section_output)[None],
        jnp.where(section == 15, zero, input_grad)[None],
    )


def solution(mesh):
    placed = (
        P("section", "seq", None),
        P("section", "seq", None),
        P("section", "seq", None),
        P(),
        P(),
        P("section", None),
        P("section", None, "seq"),
        P("section", None, "seq"),
        P("section", None, "seq"),
    )
    return jax.shard_map(
        body,
        mesh=mesh,
        in_specs=placed,
        out_specs=(P("section", "seq", None), P("section", "seq", None)),
        check_vma=False,
    )
```
